32 devices in a mesh: shot: 4 (over y, x), tile: 8 (over z, core).
Axes of the slice: x: 2, y: 2, z: 4, core: 2. Of those that a mesh axis runs over, the one named last changes fastest.
Arguments:
- p_now: float32 [4, 1024, 16, 128], P('shot', 'tile'), may hold values from -6 to 6
- p_prev: float32 [4, 1024, 16, 128], P('shot', 'tile'), may hold values from -6 to 6
- adj_now: float32 [4, 1024, 16, 128], P('shot', 'tile'), may hold values from -60 to 60
- adj_next: float32 [4, 1024, 16, 128], P('shot', 'tile'), may hold values from -60 to 60
- coef_old: float32 [512, 512], P('tile'), may hold values from 0.14 to 0.28
- signs: int32 [4, 512], P('shot', 'tile'), may hold values from 0 to 1
- elem_index: int32 [512], P('tile'), may hold values from 0 to 262143
- wavelet: float32 [5], replicated, may hold values from -4 to 4
Outputs:
- direction: float32 [512, 512], P('tile')
- p_last: float32 [4, 1024, 16, 128], P('shot', 'tile')
The draws below stay inside these ranges and needn't reach their ends.
All inputs are finite; a program needn't handle non-finite values.
Results may differ from the reference program's by a relative error of at most 0.0003.
Values sent between devices are 32-bit elements; how exact they have to be, the bound alone decides.
A program may use at most 64 MiB of HBM per device.

```python
import jax
import jax.numpy as jnp
from jax import lax

CX = 128
CZ = 128
CY = 16
OV = 8
STEPS = 4
ELEM_DEV = 64
CXC = 64
CYC = 8
CZC = 64
NX = 1024
NXC = 512
GROUPS = 4
ELEMS = 512
N_TILE = 8


def adjoint_field(key):
    position = jnp.arange(NX, dtype=jnp.float32) / max(NX - 1, 1)
    shape = (GROUPS, NX, CY, CZ)
    base = jnp.clip(jax.random.normal(key, shape, jnp.float32), -4.0, 4.0)
    scale = jnp.exp(jnp.log(4.0) * position)[:, None, None] * jnp.ones((1, 1, CZ), jnp.float32)
    return base * scale[None]


def draw_adj_now(key, part):
    return adjoint_field(jax.random.fold_in(key, 11))


def draw_adj_next(key, part):
    return adjoint_field(jax.random.fold_in(key, 12))


def plant(values, rng, least, high):
    place = [jax.random.randint(jax.random.fold_in(rng, axis), (), 0, length) for axis, length in enumerate(values.shape)]
    main_axis = values.shape.index(max(values.shape))
    beside = place[:main_axis] + [(place[main_axis] + 1) % values.shape[main_axis]] + place[main_axis + 1:]
    return values.at[tuple(place)].set(least).at[tuple(beside)].set(high)


def shard_levels(key, dims, shards, smallest, largest):
    def one(dim, blocks):
        steps = jax.random.uniform(jax.random.fold_in(jax.random.fold_in(key, 6), dim), (blocks,), jnp.float32, smallest / len(shards), largest / len(shards))
        return jnp.repeat(jnp.exp(steps), dims[dim] // blocks).reshape((-1,) + (1,) * (len(dims) - dim - 1))

    loudness = one(*shards[0])
    for cut in shards[1:]:
        loudness = loudness * one(*cut)
    return loudness


def bell_draw(stream_key, dims, spread, bound, split=(), kind=jnp.bfloat16):
    array = jax.random.normal(stream_key, dims, jnp.float32) * spread
    if len(split) > 0:
        array = shard_levels(stream_key, dims, split, -0.22, 0.18) * array
    return jnp.clip(array, min=-bound, max=bound).astype(kind)


def setup_inputs(seed: int = 0) -> dict:
    key_of = jax.random.split(jax.random.key(seed), 9)
    return {
        "p_now": bell_draw(key_of[0], (GROUPS, NX, CY, CZ), 1.0, 6.0, ((0, 4), (1, 8)), jnp.float32),
        "p_prev": bell_draw(key_of[1], (GROUPS, NX, CY, CZ), 1.0, 6.0, ((0, 4), (1, 8)), jnp.float32),
        "adj_now": draw_adj_now(jax.random.fold_in(key_of[8], 71), 0),
        "adj_next": draw_adj_next(jax.random.fold_in(key_of[8], 71), 0),
        "coef_old": jnp.clip(0.14 + 0.14 * jax.random.uniform(key_of[4], (NXC, CYC * CZC), jnp.float32) ** shard_levels(key_of[4], (NXC, CYC * CZC), ((0, 8),), -0.2, 0.2), 0.14, 0.28),
        "signs": plant(jax.random.randint(key_of[5], (GROUPS, ELEMS), 0, 2), jax.random.fold_in(key_of[5], 1), 0, 1).astype(jnp.int32),
        "elem_index": plant(jax.random.randint(key_of[6], (ELEMS,), 0, CX * CY * CZ), jax.random.fold_in(key_of[6], 1), 0, (CX * CY * CZ) - 1).astype(jnp.int32),
        "wavelet": bell_draw(key_of[7], (STEPS + 1,), 1.0, 4.0, (), jnp.float32),
    }


HIGH = lax.Precision.HIGHEST
LEARN = 0.02
EPSILON = 1e-06

def spectral_second(length):
    index = jnp.arange(length, dtype=jnp.int32)
    phase = index[:, None] * index[None, :] % length
    angle = 2.0 * jnp.pi / length * phase.astype(jnp.float32)
    number = jnp.minimum(index, length - index).astype(jnp.float32) * (2.0 * jnp.pi / length)
    weight = -(number * number) / length
    cosine = jnp.cos(angle)
    sine = jnp.sin(angle)
    first = jnp.dot(cosine * weight[None, :], cosine, precision=HIGH, preferred_element_type=jnp.float32)
    second = jnp.dot(sine * weight[None, :], sine, precision=HIGH, preferred_element_type=jnp.float32)
    return first + second

def taper_bell(inner, margin):
    ramp = jnp.sin(0.5 * jnp.pi * (jnp.arange(margin, dtype=jnp.float32) + 0.5) / margin) ** 2
    return jnp.concatenate([ramp, jnp.ones((inner,), jnp.float32), ramp[::-1]])

def spline_weight(offset):
    mag = jnp.abs(offset)
    inner = 2.0 / 3.0 - mag * mag + 0.5 * mag * mag * mag
    outer = (2.0 - mag) ** 3 / 6.0
    return jnp.where(mag < 1.0, inner, jnp.where(mag < 2.0, outer, 0.0))

def spline_expand_x(fine, coarse):
    rows = jnp.arange(fine, dtype=jnp.int32)[:, None]
    cols = jnp.arange(coarse + 4, dtype=jnp.int32)[None, :] - 2
    return spline_weight(((rows - 2 * cols).astype(jnp.float32) - 0.5) * 0.5)

def spline_project_x(fine, coarse):
    rows = jnp.arange(coarse, dtype=jnp.int32)[:, None]
    cols = jnp.arange(fine + 8, dtype=jnp.int32)[None, :] - 4
    return spline_weight(((cols - 2 * rows).astype(jnp.float32) - 0.5) * 0.5)

def periodic_spline(fine, coarse):
    rows = jnp.arange(fine, dtype=jnp.int32)[:, None]
    cols = jnp.arange(coarse, dtype=jnp.int32)[None, :]
    summed = jnp.zeros((fine, coarse), jnp.float32)
    for image in range(-2, 3):
        summed = summed + spline_weight(((rows - 2 * cols + image * fine).astype(jnp.float32) - 0.5) * 0.5)
    return summed

def laplacian(rimmed, field, second_x, second_z, bell):
    window = rimmed * bell[:, None, None]
    along_x = jnp.einsum('iw,wyz->iyz', second_x, window, precision=HIGH)
    along_z = jnp.einsum('xyz,zk->xyk', field, second_z, precision=HIGH)
    along_y = jnp.roll(field, 1, 1) + jnp.roll(field, -1, 1) - 2.0 * field
    return along_x + along_y + along_z

def expand_local(coef_rim):
    expander = spline_expand_x(CX, CXC)
    wide = jnp.dot(expander, coef_rim, precision=HIGH, preferred_element_type=jnp.float32).reshape(CX, CYC, CZC)
    wide = jnp.einsum('xjk,yj->xyk', wide, periodic_spline(CY, CYC), precision=HIGH)
    return jnp.einsum('xyk,zk->xyz', wide, periodic_spline(CZ, CZC), precision=HIGH)

def project_fine(rimmed):
    projector = spline_project_x(CX, CXC)
    narrow = jnp.dot(projector, rimmed.reshape(CX + 8, CY * CZ), precision=HIGH, preferred_element_type=jnp.float32)
    narrow = narrow.reshape(CXC, CY, CZ)
    narrow = jnp.einsum('xyz,yj->xjz', narrow, periodic_spline(CY, CYC), precision=HIGH)
    narrow = jnp.einsum('xjz,zk->xjk', narrow, periodic_spline(CZ, CZC), precision=HIGH)
    return narrow.reshape(CXC, CYC * CZC)

def reference(p_now, p_prev, adj_now, adj_next, coef_old, signs, elem_index, wavelet):
    second_x = spectral_second(CX + 2 * OV)[OV:OV + CX]
    second_z = spectral_second(CZ)
    bell = taper_bell(CX, OV)
    tiles = jnp.arange(N_TILE, dtype=jnp.int32)
    offsets = (tiles[:, None] * (CX * CY * CZ) + elem_index.reshape(N_TILE, ELEM_DEV)).reshape(-1).astype(jnp.int32)

    def laplace_all(field):
        padded = jnp.pad(field, ((OV, OV), (0, 0), (0, 0)))

        def one_tile(tile):
            rimmed = lax.dynamic_slice_in_dim(padded, tile * CX, CX + 2 * OV, 0)
            core = lax.dynamic_slice_in_dim(field, tile * CX, CX, 0)
            return laplacian(rimmed, core, second_x, second_z, bell)
        return lax.map(one_tile, tiles).reshape(field.shape)

    def expand_all(coef):
        padded = jnp.pad(coef, ((2, 2), (0, 0)))

        def one_tile(tile):
            return expand_local(lax.dynamic_slice_in_dim(padded, tile * CXC, CXC + 4, 0))
        return lax.map(one_tile, tiles).reshape(NX, CY, CZ)

    def project_all(image):
        padded = jnp.pad(image, ((4, 4), (0, 0), (0, 0)))

        def one_tile(tile):
            return project_fine(lax.dynamic_slice_in_dim(padded, tile * CX, CX + 8, 0))
        return lax.map(one_tile, tiles).reshape(NXC, CYC * CZC)

    def inject(field, step, amounts):
        flat = field.reshape(-1).at[offsets].add(wavelet[step] * amounts)
        return flat.reshape(field.shape)
    speed_old = expand_all(coef_old)
    squared_old = speed_old * speed_old

    def one_group(inputs):
        field_now, field_prev, adjoint_now, adjoint_next, sign_row = inputs
        amounts = (2 * sign_row - 1).astype(jnp.float32)
        forward = [field_prev, field_now]
        curvatures = []
        for step in range(STEPS):
            lap_p = laplace_all(forward[-1])
            curvatures.append(lap_p)
            following = 2.0 * forward[-1] - forward[-2] + squared_old * lap_p
            forward.append(inject(following, step, amounts))
        adjoint = [adjoint_next, adjoint_now]
        for step in range(STEPS):
            lap_q = laplace_all(adjoint[-1])
            adjoint.append(2.0 * adjoint[-1] - adjoint[-2] + squared_old * lap_q)
        summed = jnp.zeros_like(field_now)
        for step in range(STEPS):
            summed = summed + adjoint[STEPS + 1 - step] * curvatures[step]
        image = 2.0 * speed_old * summed
        return (project_all(image), forward[-2], forward[-1])
    partials, third, fourth = lax.map(one_group, (p_now, p_prev, adj_now, adj_next, signs))
    total = lax.optimization_barrier(jnp.sum(partials, axis=0))
    scale = jnp.sqrt(jnp.sum(total * total) / (NXC * CYC * CZC) + EPSILON)
    direction = total / scale
    coef_new = coef_old - LEARN * direction
    speed_new = expand_all(coef_new)
    squared_new = speed_new * speed_new

    def last_step(inputs):
        before, latest, sign_row = inputs
        amounts = (2 * sign_row - 1).astype(jnp.float32)
        following = 2.0 * latest - before + squared_new * laplace_all(latest)
        return inject(following, STEPS, amounts)
    p_last = lax.map(last_step, (third, fourth, signs))
    return (direction, p_last)
```

```python
import functools

import jax
import jax.numpy as jnp
import ml_dtypes
import numpy as np
from jax import lax
from jax.experimental import pallas as pl
from jax.experimental.pallas import tpu as pltpu
from jax.sharding import PartitionSpec as P

OV = 8
LEARN = 0.02
EPSILON = 1e-06
F32 = jnp.float32
BF16 = jnp.bfloat16
MESH = pl.DeviceIdType.MESH


def spectral_second(length):
    index = np.arange(length)
    number = np.minimum(index, length - index) * (2.0 * np.pi / length)
    gap = (index[:, None] - index[None, :])[:, :, None] * index[None, None, :] % length
    return np.sum(-(number * number) / length * np.cos(2.0 * np.pi / length * gap), axis=-1)


def spline_weight(offset):
    mag = np.abs(offset)
    inner = 2.0 / 3.0 - mag * mag + 0.5 * mag * mag * mag
    outer = (2.0 - mag) ** 3 / 6.0
    return np.where(mag < 1.0, inner, np.where(mag < 2.0, outer, 0.0))


def periodic_spline(fine, coarse):
    gap = np.arange(fine)[:, None] - 2 * np.arange(coarse)[None, :]
    return sum(spline_weight((gap + image * fine - 0.5) * 0.5) for image in range(-2, 3))


def halves(matrix):
    high = matrix.astype(np.float32).astype(ml_dtypes.bfloat16)
    low = (matrix - high.astype(np.float64)).astype(ml_dtypes.bfloat16)
    return high, low


def twice(block):
    out = np.zeros((2 * block.shape[0], 2 * block.shape[1]))
    out[: block.shape[0], : block.shape[1]] = block
    out[block.shape[0] :, block.shape[1] :] = block
    return out


def constants(cx, cz, cxc, czc):
    full = cx + 2 * OV
    ramp = np.sin(0.5 * np.pi * (np.arange(OV) + 0.5) / OV) ** 2
    second_x = spectral_second(full)[OV : OV + cx]
    high, low = halves(second_x[:, OV : OV + cx] - 2.0 * np.eye(cx))
    rim = np.concatenate([second_x[:, :OV] * ramp, second_x[:, OV + cx :] * ramp[::-1]], 1)
    rim_high, rim_low = halves(rim)
    core_x = np.concatenate([high, high, low, rim_high, rim_high, rim_low, rim_low], 1)
    high, low = halves(spectral_second(cz))
    core_z = np.block([[high, low], [high, low]])
    gap = np.arange(cx)[:, None] - 2 * (np.arange(cxc + 2 * OV)[None, :] - OV)
    expand_x = spline_weight((gap - 0.5) * 0.5)
    spline_z = periodic_spline(cz, czc)
    floats = [expand_x, twice(spline_z.T), expand_x.T, twice(spline_z)]
    return [core_x, core_z] + [m.astype(np.float32) for m in floats]


def split(value):
    high = value.astype(BF16)
    return high, (value - high.astype(F32)).astype(BF16)


def dot(a, b):
    return jnp.dot(a, b, preferred_element_type=F32)


def dot3(a, b):
    ah, al = split(a)
    bh, bl = split(b)
    return dot(ah, bh) + (dot(ah, bl) + dot(al, bh))


def kernel(
    dims, n_shot, n_tile, spline_y,
    p_now, p_prev, q_now, q_next, coef_in, signs, elems, wave,
    core_x_in, core_z_in, exp_x_in, exp_z_in, pro_x_in, pro_z_in,
    direction, p_last,
    raw, raw_sem, pf, qf, lp, dp, dq, sig, sig2, src, wide, exp_t,
    ph, qh, cext, narrow, part0, rims, part, rs, tot, ttot, sq_out, sq_in,
    ph_s, ph_r, qh_s, qh_r, ce_s, ce_r, ri_s, ri_r, rs_s, rs_r, ag_s, ag_r, sq_s, sq_r,
    sq_all, sa_s, sa_r, consts_sem, coef, core_x, core_z, exp_x, exp_z, pro_x, pro_z,
):
    cx, cy, cz, cxc, pairs, steps, group, rows = dims
    shot = lax.axis_index("shot")
    tile = lax.axis_index("tile")
    has_left = tile > 0
    has_right = tile < n_tile - 1
    ext = cxc + 2 * OV

    barrier = pltpu.get_barrier_semaphore()
    for d in range(1, n_tile):
        pl.semaphore_signal(
            barrier, inc=1, device_id={"tile": lax.rem(tile + d, n_tile)}, device_id_type=MESH
        )
    for d in range(1, n_shot):
        pl.semaphore_signal(
            barrier, inc=1, device_id={"shot": lax.rem(shot + d, n_shot)}, device_id_type=MESH
        )

    def load(ref, out, s):
        copy = pltpu.make_async_copy(ref, out, s)
        copy.start()
        return copy

    fields = (p_now, q_now, p_prev, q_next)
    matrices = (
        (core_x_in, core_x), (core_z_in, core_z), (exp_x_in, exp_x),
        (exp_z_in, exp_z), (pro_x_in, pro_x), (pro_z_in, pro_z),
    )
    loads = [load(fields[0], raw.at[0], raw_sem.at[0])]
    coef_load = load(coef_in, coef, consts_sem.at[0])
    loads.append(load(fields[1], raw.at[1], raw_sem.at[1]))
    matrix_loads = [load(a, b, consts_sem.at[i + 1]) for i, (a, b) in enumerate(matrices)]
    loads += [load(fields[i], raw.at[i], raw_sem.at[i]) for i in (2, 3)]

    def to_planes(i, out):
        loads[i].wait()
        for y in range(cy):
            out[y] = raw[i, pl.ds(y, cx, stride=cy), :]

    def to_steps(i, now, out):
        loads[i].wait()
        for y in range(cy):
            out[y] = now[y] - raw[i, pl.ds(y, cx, stride=cy), :]

    @pl.when(jnp.logical_not(has_left))
    def _():
        ph[:, 0] = jnp.zeros_like(ph[:, 0])
        qh[:, 0] = jnp.zeros_like(qh[:, 0])
        cext[:, :OV, :] = jnp.zeros((pairs, OV, 128), F32)
        rims[0] = jnp.zeros_like(rims[0])

    @pl.when(jnp.logical_not(has_right))
    def _():
        ph[:, 1] = jnp.zeros_like(ph[:, 1])
        qh[:, 1] = jnp.zeros_like(qh[:, 1])
        cext[:, OV + cxc :, :] = jnp.zeros((pairs, OV, 128), F32)
        rims[1] = jnp.zeros_like(rims[1])

    def beside(to_right, right_dst, to_left, left_dst, ss, rr):
        right = pltpu.make_async_remote_copy(
            src_ref=to_right, dst_ref=right_dst, send_sem=ss.at[0], recv_sem=rr.at[0],
            device_id={"tile": lax.rem(tile + 1, n_tile)}, device_id_type=MESH,
        )
        left = pltpu.make_async_remote_copy(
            src_ref=to_left, dst_ref=left_dst, send_sem=ss.at[1], recv_sem=rr.at[1],
            device_id={"tile": lax.rem(tile + n_tile - 1, n_tile)}, device_id_type=MESH,
        )
        return right, left

    def start(pair):
        @pl.when(has_right)
        def _():
            pair[0].start()

        @pl.when(has_left)
        def _():
            pair[1].start()

    def finish(pair):
        @pl.when(has_right)
        def _():
            pair[0].wait_send()
            pair[1].wait_recv()

        @pl.when(has_left)
        def _():
            pair[1].wait_send()
            pair[0].wait_recv()

    def field_halo(field, index, halo, t, ss, rr):
        return beside(
            field.at[index, :, cx - OV :, :], halo.at[t, 0],
            field.at[index, :, :OV, :], halo.at[t, 1], ss.at[t], rr.at[t],
        )

    p_halo = lambda t: field_halo(pf, t + 1, ph, t, ph_s, ph_r)
    q_halo = lambda t: field_halo(qf, t + 1, qh, t, qh_s, qh_r)

    to_planes(0, pf.at[1])
    pl.semaphore_wait(barrier, n_tile + n_shot - 2)
    start(p_halo(0))
    to_planes(1, qf.at[1])
    start(q_halo(0))
    coef_load.wait()
    for a in range(pairs):
        cext[a, OV : OV + cxc, :] = coef[:, a * 128 : (a + 1) * 128]
    coef_rims = beside(
        cext.at[:, cxc : cxc + OV, :], cext.at[:, :OV, :],
        cext.at[:, OV : 2 * OV, :], cext.at[:, OV + cxc :, :], ce_s, ce_r,
    )
    start(coef_rims)

    def laplace(field, halo, use):
        for i in range(cy // 2):
            y0, y1 = 2 * i, 2 * i + 1
            a = field[y0]
            b = field[y1]
            high, low = split(jnp.concatenate([a, b], 1))
            edge = jnp.concatenate(
                [
                    jnp.concatenate([halo[0, y0], halo[0, y1]], 1),
                    jnp.concatenate([halo[1, y0], halo[1, y1]], 1),
                ],
                0,
            )
            eh, el = split(edge)
            ox = dot(core_x[...], jnp.concatenate([high, low, high, eh, el, eh, el], 0))
            oz = dot(
                jnp.concatenate(
                    [
                        jnp.concatenate([high[:, :cz], low[:, :cz]], 1),
                        jnp.concatenate([high[:, cz:], low[:, cz:]], 1),
                    ],
                    0,
                ),
                core_z[...],
            )
            before = field[(y0 + cy - 1) % cy]
            after = field[(y1 + 1) % cy]
            oz = oz[:, :cz] + oz[:, cz:]
            use(y0, a, ox[:, :cz] + oz[:cx] + (before + b))
            use(y1, b, ox[:, cz:] + oz[cx:] + (a + after))

    def expand(coefs, out):
        for a in range(pairs):
            both = dot3(dot3(exp_x[...], coefs[a]), exp_z[...])
            wide[2 * a] = both[:, :cz]
            wide[2 * a + 1] = both[:, cz:]

        def body(i, carry):
            at = pl.ds(pl.multiple_of(i * 8, 8), 8)
            planes = [wide[j, at, :] for j in range(2 * pairs)]
            for y in range(cy):
                terms = [
                    float(spline_y[y, j]) * planes[j] for j in range(2 * pairs) if spline_y[y, j] != 0
                ]
                out[y, at, :] = functools.reduce(lambda u, v: u + v, terms)
            return carry

        lax.fori_loop(0, cx // 8, body, 0)

    count = elems.shape[1]
    where_to = elems[...]
    amount = (2 * signs[...] - 1).astype(F32)
    row_of = lax.rem(lax.div(where_to, cz), cy) * cx + lax.div(where_to, cz * cy)
    lanes = (lax.broadcasted_iota(jnp.int32, (cz, count), 0) == lax.rem(where_to, cz)).astype(F32)
    lanes = lanes.astype(BF16)

    def source(y, carry):
        place = lax.broadcasted_iota(jnp.int32, (cx, count), 0) + y * cx
        hits = jnp.where(place == row_of, amount, 0.0).astype(BF16)
        src[y] = lax.dot_general(hits, lanes, (((1,), (1,)), ((), ())), preferred_element_type=F32)
        return carry

    lax.fori_loop(0, cy, source, 0, unroll=2)
    to_steps(2, pf.at[1], dp)
    to_steps(3, qf.at[1], dq)
    for copy in matrix_loads:
        copy.wait()
    finish(coef_rims)
    expand(cext, sig)

    def square(y, carry):
        value = sig[y]
        sig2[y] = value * value
        return carry

    lax.fori_loop(0, cy, square, 0)

    for t in range(steps):
        finish(p_halo(t))
        scale = wave[t]

        def use_p(y, now, lap):
            lp[t, y] = lap
            moved = dp[y] + sig2[y] * lap + scale * src[y]
            dp[y] = moved
            pf[t + 2, y] = now + moved

        laplace(pf.at[t + 1], ph.at[t], use_p)
        start(p_halo(t + 1))
        finish(q_halo(t))

        def use_q(y, now, lap):
            moved = dq[y] + sig2[y] * lap
            dq[y] = moved
            qf[t + 2, y] = now + moved

        laplace(qf.at[t + 1], qh.at[t], use_q)
        if t < steps - 1:
            start(q_halo(t + 1))

    def image(i, carry):
        at = pl.ds(pl.multiple_of(i * 8, 8), 8)
        out = [None] * (2 * pairs)
        for y in range(cy):
            summed = qf[steps + 1, y, at, :] * lp[0, y, at, :]
            for t in range(1, steps):
                summed = summed + qf[steps + 1 - t, y, at, :] * lp[t, y, at, :]
            value = 2.0 * sig[y, at, :] * summed
            for j in range(2 * pairs):
                if spline_y[y, j] != 0:
                    term = float(spline_y[y, j]) * value
                    out[j] = term if out[j] is None else out[j] + term
        for j in range(2 * pairs):
            narrow[j, at, :] = out[j]
        return carry

    lax.fori_loop(0, cx // 8, image, 0)
    for a in range(pairs):
        both = jnp.concatenate([narrow[2 * a], narrow[2 * a + 1]], 1)
        part0[a] = dot3(dot3(pro_x[...], both), pro_z[...])
    part_rims = beside(
        part0.at[:, cxc:, :], rims.at[0], part0.at[:, : 2 * OV, :], rims.at[1], ri_s, ri_r
    )
    start(part_rims)
    finish(part_rims)
    halfs = ext // rows
    for a in range(pairs):
        whole = jnp.concatenate(
            [
                part0[a, : 2 * OV, :] + rims[0, a],
                part0[a, 2 * OV : cxc, :],
                part0[a, cxc:, :] + rims[1, a],
            ],
            0,
        )
        for r in range(halfs):
            flat = a * halfs + r
            part[flat // group, flat % group] = whole[r * rows : (r + 1) * rows]

    def peer_copy(source_ref, target_ref, d, ss, rr):
        return pltpu.make_async_remote_copy(
            src_ref=source_ref, dst_ref=target_ref, send_sem=ss.at[d - 1], recv_sem=rr.at[d - 1],
            device_id={"shot": lax.rem(shot + d, n_shot)}, device_id_type=MESH,
        )

    scatter = []
    for d in range(1, n_shot):
        copy = peer_copy(part.at[lax.rem(shot + d, n_shot)], rs.at[d - 1], d, rs_s, rs_r)
        copy.start()
        scatter.append(copy)
    finish(p_halo(steps))

    def keep_lap(y, now, lap):
        lp[steps, y] = lap

    laplace(pf.at[steps + 1], ph.at[steps], keep_lap)
    mine = part[shot]
    for d in range(1, n_shot):
        scatter[d - 1].wait()
        mine = mine + rs[d - 1]
    tot[shot] = mine
    gather = []
    for d in range(1, n_shot):
        copy = peer_copy(tot.at[shot], tot.at[shot], d, ag_s, ag_r)
        copy.start()
        gather.append(copy)
    squares = jnp.zeros((8, 128), F32)
    first = lax.rem(shot, halfs) * rows
    for g in range(group):
        for r in range(0, rows, 8):
            inside = jnp.logical_and(first + r >= OV, first + r < OV + cxc)
            value = mine[g, r : r + 8] * jnp.where(inside, 1.0, 0.0).astype(F32)
            squares = squares + value * mine[g, r : r + 8]
    sq_out[...] = squares
    sums = []
    for d in range(1, n_tile):
        copy = pltpu.make_async_remote_copy(
            src_ref=sq_out, dst_ref=sq_in.at[d - 1], send_sem=sq_s.at[d - 1], recv_sem=sq_r.at[d - 1],
            device_id={"tile": lax.rem(tile + d, n_tile)}, device_id_type=MESH,
        )
        copy.start()
        sums.append(copy)
    for d in range(1, n_tile):
        sums[d - 1].wait()
        squares = squares + sq_in[d - 1]
    sq_all[shot] = squares
    sums = []
    for d in range(1, n_shot):
        copy = peer_copy(sq_all.at[shot], sq_all.at[shot], d, sa_s, sa_r)
        copy.start()
        sums.append(copy)
    for copy in gather:
        copy.wait()
    left_on = jnp.where(has_left, 1.0, 0.0).astype(F32)
    right_on = jnp.where(has_right, 1.0, 0.0).astype(F32)
    for a in range(pairs):
        pieces = []
        for r in range(halfs):
            flat = a * halfs + r
            pieces.append(tot[flat // group, flat % group])
        whole = pieces[0] if halfs == 1 else jnp.concatenate(pieces, 0)
        ttot[a, :OV, :] = whole[:OV] * left_on
        ttot[a, OV : OV + cxc, :] = whole[OV : OV + cxc]
        ttot[a, OV + cxc :, :] = whole[OV + cxc :] * right_on
    expand(ttot, exp_t)
    for copy in sums:
        copy.wait()
    squares = sq_all[0]
    for d in range(1, n_shot):
        squares = squares + sq_all[d]
    cells = float(n_tile * cxc * 2 * pairs * 64)
    mean = jnp.sum(jnp.sum(squares, axis=0, keepdims=True), axis=1, keepdims=True) / cells
    scale = 1.0 / jnp.sqrt(mean + EPSILON)
    for a in range(pairs):
        direction[:, a * 128 : (a + 1) * 128] = ttot[a, OV : OV + cxc, :] * scale
    moved = LEARN * scale
    last = wave[steps]
    for y in range(cy):
        speed = sig[y] - moved * exp_t[y]
        p_last[pl.ds(y, cx, stride=cy), :] = (
            pf[steps + 1, y] + dp[y] + speed * speed * lp[steps, y] + last * src[y]
        )


def on_device(n_shot, n_tile, p_now, p_prev, adj_now, adj_next, coef_old, signs, elem_index, wavelet):
    _, cx, cy, cz = p_now.shape
    cxc, merged = coef_old.shape
    steps = wavelet.shape[0] - 1
    cyc = cy // 2
    czc = merged // cyc
    pairs = cyc // 2
    spline_y = periodic_spline(cy, cyc).astype(np.float32)
    ext = cxc + 2 * OV
    group = max(1, pairs // n_shot)
    rows = ext // max(1, n_shot // pairs)
    dims = (cx, cy, cz, cxc, pairs, steps, group, rows)
    flat = lambda v: v.reshape(cx * cy, cz)
    consts = [jnp.asarray(c) for c in constants(cx, cz, cxc, czc)]
    vmem = pl.BlockSpec(memory_space=pltpu.VMEM)
    held = lambda v: pltpu.with_memory_space_constraint(v, pltpu.HBM)
    field = (cy, cx, cz)
    buf = lambda *shape: pltpu.VMEM(shape, F32)
    sem = lambda *shape: pltpu.SemaphoreType.DMA(shape)
    direction, p_last = pl.pallas_call(
        functools.partial(kernel, dims, n_shot, n_tile, spline_y),
        out_shape=(
            jax.ShapeDtypeStruct((cxc, merged), F32),
            jax.ShapeDtypeStruct((cx * cy, cz), F32),
        ),
        in_specs=[pl.BlockSpec(memory_space=pltpu.HBM)] * 5
        + [vmem] * 2
        + [pl.BlockSpec(memory_space=pltpu.SMEM)]
        + [pl.BlockSpec(memory_space=pltpu.HBM)] * len(consts),
        out_specs=(vmem, vmem),
        scratch_shapes=[
            buf(4, cx * cy, cz), sem(4),
            buf(steps + 2, *field), buf(steps + 2, *field), buf(steps + 1, *field), buf(*field), buf(*field),
            buf(*field), buf(*field), buf(*field), buf(cyc, cx, cz), buf(*field),
            buf(steps + 1, 2, cy, OV, cz), buf(steps, 2, cy, OV, cz),
            buf(pairs, ext, 128), buf(cyc, cx, cz), buf(pairs, ext, 128),
            buf(2, pairs, 2 * OV, 128),
            buf(n_shot, group, rows, 128), buf(max(1, n_shot - 1), group, rows, 128),
            buf(n_shot, group, rows, 128), buf(pairs, ext, 128),
            buf(8, 128), buf(max(1, n_tile - 1), 8, 128),
            sem(steps + 1, 2), sem(steps + 1, 2), sem(steps, 2), sem(steps, 2),
            sem(2), sem(2), sem(2), sem(2),
            sem(max(1, n_shot - 1)), sem(max(1, n_shot - 1)),
            sem(max(1, n_shot - 1)), sem(max(1, n_shot - 1)),
            sem(max(1, n_tile - 1)), sem(max(1, n_tile - 1)),
            buf(n_shot, 8, 128), sem(max(1, n_shot - 1)), sem(max(1, n_shot - 1)),
            sem(1 + len(consts)), buf(cxc, merged),
        ]
        + [pltpu.VMEM(c.shape, c.dtype) for c in consts],
        compiler_params=pltpu.CompilerParams(
            collective_id=0, has_side_effects=True, vmem_limit_bytes=38 * 1024 * 1024
        ),
    )(
        *map(held, (flat(p_now), flat(p_prev), flat(adj_now), flat(adj_next), coef_old)),
        signs, elem_index.reshape(1, -1), wavelet, *map(held, consts),
    )
    return direction, p_last.reshape(1, cx, cy, cz)


def solution(mesh):
    placed = (
        P("shot", "tile", None, None),
        P("shot", "tile", None, None),
        P("shot", "tile", None, None),
        P("shot", "tile", None, None),
        P("tile", None),
        P("shot", "tile"),
        P("tile"),
        P(),
    )
    return jax.shard_map(
        functools.partial(on_device, mesh.shape["shot"], mesh.shape["tile"]),
        mesh=mesh,
        in_specs=placed,
        out_specs=(P("tile", None), P("shot", "tile", None, None)),
        check_vma=False,
    )
```

```python
import functools

import jax
import jax.numpy as jnp
import ml_dtypes
import numpy as np
from jax import lax
from jax.experimental import pallas as pl
from jax.experimental.pallas import tpu as pltpu
from jax.sharding import PartitionSpec as P

OV = 8
CHUNKS = 2
LEARN = 0.02
EPSILON = 1e-06
F32 = jnp.float32
BF16 = jnp.bfloat16
MESH = pl.DeviceIdType.MESH


def spectral_second(length):
    index = np.arange(length)
    number = np.minimum(index, length - index) * (2.0 * np.pi / length)
    gap = (index[:, None] - index[None, :])[:, :, None] * index[None, None, :] % length
    return np.sum(-(number * number) / length * np.cos(2.0 * np.pi / length * gap), axis=-1)


def spline_weight(offset):
    mag = np.abs(offset)
    inner = 2.0 / 3.0 - mag * mag + 0.5 * mag * mag * mag
    outer = (2.0 - mag) ** 3 / 6.0
    return np.where(mag < 1.0, inner, np.where(mag < 2.0, outer, 0.0))


def periodic_spline(fine, coarse):
    gap = np.arange(fine)[:, None] - 2 * np.arange(coarse)[None, :]
    return sum(spline_weight((gap + image * fine - 0.5) * 0.5) for image in range(-2, 3))


def halves(matrix):
    high = matrix.astype(np.float32).astype(ml_dtypes.bfloat16)
    low = (matrix - high.astype(np.float64)).astype(ml_dtypes.bfloat16)
    return high, low


def twice(block):
    out = np.zeros((2 * block.shape[0], 2 * block.shape[1]))
    out[: block.shape[0], : block.shape[1]] = block
    out[block.shape[0] :, block.shape[1] :] = block
    return out


def constants(cx, cz, cxc, czc):
    full = cx + 2 * OV
    ramp = np.sin(0.5 * np.pi * (np.arange(OV) + 0.5) / OV) ** 2
    second_x = spectral_second(full)[OV : OV + cx]
    high, low = halves(second_x[:, OV : OV + cx] - 2.0 * np.eye(cx))
    rim = np.concatenate([second_x[:, :OV] * ramp, second_x[:, OV + cx :] * ramp[::-1]], 1)
    rim_high, rim_low = halves(rim)
    core_x = np.concatenate([high, high, low, rim_high, rim_high, rim_low, rim_low], 1)
    high, low = halves(spectral_second(cz))
    core_z = np.block([[high, low], [high, low]])
    gap = np.arange(cx)[:, None] - 2 * (np.arange(cxc + 2 * OV)[None, :] - OV)
    expand_x = spline_weight((gap - 0.5) * 0.5)
    spline_z = periodic_spline(cz, czc)
    across = lambda m: np.concatenate([*(halves(m)[:1] * 2), halves(m)[1]], 1)
    down = lambda m: np.concatenate([*(halves(m)[:1] * 2), halves(m)[1]], 0)
    return [core_x, core_z, across(expand_x), down(twice(spline_z.T)), across(expand_x.T), down(twice(spline_z))]


def split(value):
    high = value.astype(BF16)
    return high, (value - high.astype(F32)).astype(BF16)


def dot(a, b):
    return jnp.dot(a, b, preferred_element_type=F32)


def kernel(
    dims, n_shot, n_tile, spline_y,
    p_now, p_prev, q_now, q_next, coef_in, signs_in, elems_in, wave_in,
    core_x_in, core_z_in, exp_x_in, exp_z_in, pro_x_in, pro_z_in,
    base, lap_last, sig, exp_t, ttot, scale_out,
    raw_sem, pf, qf, pv, qv, lp, dp, dq, acc, sig2, src, wide,
    ph, qh, cext, narrow, part0, rims, rs, tot, sq_all,
    ph_s, ph_r, qh_s, qh_r, ce_s, ce_r, ri_s, ri_r, rs_s, rs_r, ag_s, ag_r, sq_s, sq_r,
    tile_sem, shot_sem, consts_sem, signs, elems, wave, coef,
    core_x, core_z, exp_x, exp_z, pro_x, pro_z,
):
    cx, cy, cz, cxc, pairs, steps, group, rows, chunks = dims
    width = cy // chunks
    shot = lax.axis_index("shot")
    tile = lax.axis_index("tile")
    has_left = tile > 0
    has_right = tile < n_tile - 1
    ext = cxc + 2 * OV

    def across(bit):
        return shot + bit - 2 * bit * lax.rem(lax.div(shot, bit), 2)

    barrier = pltpu.get_barrier_semaphore()
    bits = [1 << b for b in range((n_shot - 1).bit_length())]
    reaches = [1 << b for b in range((n_tile - 2).bit_length())]

    def greet(right, left, reach):
        @pl.when(tile < n_tile - reach)
        def _():
            pl.semaphore_signal(
                right, inc=1, device_id={"tile": lax.rem(tile + reach, n_tile)}, device_id_type=MESH
            )

        @pl.when(tile >= reach)
        def _():
            pl.semaphore_signal(
                left, inc=1, device_id={"tile": lax.rem(tile + n_tile - reach, n_tile)}, device_id_type=MESH
            )

    greet(barrier, barrier, 1)
    for bit in bits:
        pl.semaphore_signal(barrier, inc=1, device_id={"shot": across(bit)}, device_id_type=MESH)

    def tell(i):
        if i < len(reaches):
            greet(tile_sem.at[i, 0], tile_sem.at[i, 1], reaches[i])
        elif i < len(reaches) + len(bits):
            at = i - len(reaches)
            pl.semaphore_signal(shot_sem.at[at], inc=1, device_id={"shot": across(bits[at])}, device_id_type=MESH)

    def hear(i):
        if i < len(reaches):
            @pl.when(tile >= reaches[i])
            def _():
                pl.semaphore_wait(tile_sem.at[i, 0], 1)

            @pl.when(tile < n_tile - reaches[i])
            def _():
                pl.semaphore_wait(tile_sem.at[i, 1], 1)
        elif i < len(reaches) + len(bits):
            pl.semaphore_wait(shot_sem.at[i - len(reaches)], 1)

    def load(ref, out, s):
        copy = pltpu.make_async_copy(ref, out, s)
        copy.start()
        return copy

    fields = ((p_now, pf.at[1]), (q_now, qf.at[1]), (p_prev, pv), (q_next, qv))
    matrices = (
        (coef_in, coef), (signs_in, signs), (elems_in, elems), (wave_in, wave),
        (core_x_in, core_x), (core_z_in, core_z), (exp_x_in, exp_x),
        (exp_z_in, exp_z), (pro_x_in, pro_x), (pro_z_in, pro_z),
    )

    def load_planes(i):
        for y in range(cy):
            pltpu.make_async_copy(fields[i][0].at[:, y, :], fields[i][1].at[y], raw_sem.at[i]).start()

    def loaded(i):
        pltpu.make_async_copy(fields[i][1], fields[i][1], raw_sem.at[i]).wait()

    load_planes(0)
    load_planes(1)
    small = [load(a, b, consts_sem.at[i]) for i, (a, b) in enumerate(matrices)]
    load_planes(2)
    load_planes(3)

    @pl.when(jnp.logical_not(has_left))
    def _():
        ph[:, 0] = jnp.zeros_like(ph[:, 0])
        qh[:, 0] = jnp.zeros_like(qh[:, 0])
        cext[:, :OV, :] = jnp.zeros((pairs, OV, 128), F32)
        rims[0] = jnp.zeros_like(rims[0])

    @pl.when(jnp.logical_not(has_right))
    def _():
        ph[:, 1] = jnp.zeros_like(ph[:, 1])
        qh[:, 1] = jnp.zeros_like(qh[:, 1])
        cext[:, OV + cxc :, :] = jnp.zeros((pairs, OV, 128), F32)
        rims[1] = jnp.zeros_like(rims[1])

    def beside(to_right, right_dst, to_left, left_dst, ss, rr):
        right = pltpu.make_async_remote_copy(
            src_ref=to_right, dst_ref=right_dst, send_sem=ss.at[0], recv_sem=rr.at[0],
            device_id={"tile": lax.rem(tile + 1, n_tile)}, device_id_type=MESH,
        )
        left = pltpu.make_async_remote_copy(
            src_ref=to_left, dst_ref=left_dst, send_sem=ss.at[1], recv_sem=rr.at[1],
            device_id={"tile": lax.rem(tile + n_tile - 1, n_tile)}, device_id_type=MESH,
        )
        return right, left

    def start(pair):
        @pl.when(has_right)
        def _():
            pair[0].start()

        @pl.when(has_left)
        def _():
            pair[1].start()

    def finish(pair):
        @pl.when(has_right)
        def _():
            pair[0].wait_send()
            pair[1].wait_recv()

        @pl.when(has_left)
        def _():
            pair[1].wait_send()
            pair[0].wait_recv()

    def field_halo(field, index, halo, t, c, ss, rr):
        planes = pl.ds(c * width, width)
        return beside(
            field.at[index, planes, cx - OV :, :], halo.at[t, 0, planes],
            field.at[index, planes, :OV, :], halo.at[t, 1, planes], ss.at[t, c], rr.at[t, c],
        )

    p_halo = lambda t, c: field_halo(pf, t + 1, ph, t, c, ph_s, ph_r)
    q_halo = lambda t, c: field_halo(qf, t + 1, qh, t, c, qh_s, qh_r)

    def arrive(pair):
        @pl.when(has_right)
        def _():
            pair[1].wait_recv()

        @pl.when(has_left)
        def _():
            pair[0].wait_recv()

    def sent(pairs):
        @pl.when(has_right)
        def _():
            for pair in pairs:
                pair[0].wait_send()

        @pl.when(has_left)
        def _():
            for pair in pairs:
                pair[1].wait_send()

    beside_count = 1 - lax.div(tile + 1, n_tile) + lax.div(tile + n_tile - 1, n_tile)
    pl.semaphore_wait(barrier, len(bits) + beside_count)
    loaded(0)
    for c in range(chunks):
        start(p_halo(0, c))
    loaded(1)
    for c in range(chunks):
        start(q_halo(0, c))
    tell(0)
    for copy in small[:4]:
        copy.wait()
    for a in range(pairs):
        cext[a, OV : OV + cxc, :] = coef[:, a * 128 : (a + 1) * 128]
    coef_rims = beside(
        cext.at[:, cxc : cxc + OV, :], cext.at[:, :OV, :],
        cext.at[:, OV : 2 * OV, :], cext.at[:, OV + cxc :, :], ce_s, ce_r,
    )
    start(coef_rims)

    def laplace(field, halo, c, use):
        for i in range(c * width // 2, (c + 1) * width // 2):
            y0, y1 = 2 * i, 2 * i + 1
            a = field[y0]
            b = field[y1]
            high, low = split(jnp.concatenate([a, b], 1))
            edge = jnp.concatenate(
                [
                    jnp.concatenate([halo[0, y0], halo[0, y1]], 1),
                    jnp.concatenate([halo[1, y0], halo[1, y1]], 1),
                ],
                0,
            )
            eh, el = split(edge)
            ox = dot(core_x[...], jnp.concatenate([high, low, high, eh, el, eh, el], 0))
            oz = dot(
                jnp.concatenate(
                    [
                        jnp.concatenate([high[:, :cz], low[:, :cz]], 1),
                        jnp.concatenate([high[:, cz:], low[:, cz:]], 1),
                    ],
                    0,
                ),
                core_z[...],
            )
            before = field[(y0 + cy - 1) % cy]
            after = field[(y1 + 1) % cy]
            oz = oz[:, :cz] + oz[:, cz:]
            use(y0, a, ox[:, :cz] + oz[:cx] + (before + b))
            use(y1, b, ox[:, cz:] + oz[cx:] + (a + after))

    def expand(coefs, out):
        tall = []
        for a in range(0, pairs, 2):
            high, low = split(jnp.concatenate([coefs[a], coefs[a + 1]], 1))
            both = dot(exp_x[...], jnp.concatenate([high, low, high], 0))
            tall += [both[:, :128], both[:, 128:]]
        high, low = split(jnp.concatenate(tall, 0))
        both = dot(jnp.concatenate([high, low, high], 1), exp_z[...])
        for a in range(pairs):
            wide[2 * a] = both[a * cx : (a + 1) * cx, :cz]
            wide[2 * a + 1] = both[a * cx : (a + 1) * cx, cz:]

        def body(i, carry):
            at = pl.ds(pl.multiple_of(i * 8, 8), 8)
            planes = [wide[j, at, :] for j in range(2 * pairs)]
            for y in range(cy):
                terms = [
                    float(spline_y[y, j]) * planes[j] for j in range(2 * pairs) if spline_y[y, j] != 0
                ]
                out[y, at, :] = functools.reduce(lambda u, v: u + v, terms)
            return carry

        lax.fori_loop(0, cx // 8, body, 0)

    count = elems.shape[1]
    where_to = elems[...]
    amount = (2 * signs[...] - 1).astype(F32)
    row_of = lax.rem(lax.div(where_to, cz), cy) * cx + lax.div(where_to, cz * cy)
    lanes = (lax.broadcasted_iota(jnp.int32, (cz, count), 0) == lax.rem(where_to, cz)).astype(F32)
    lanes = lanes.astype(BF16)

    def source(y, carry):
        place = lax.broadcasted_iota(jnp.int32, (cx, count), 0) + y * cx
        hits = jnp.where(place == row_of, amount, 0.0).astype(BF16)
        src[y] = lax.dot_general(hits, lanes, (((1,), (1,)), ((), ())), preferred_element_type=F32)
        return carry

    lax.fori_loop(0, cy, source, 0, unroll=2)
    for copy in small[4:]:
        copy.wait()
    finish(coef_rims)
    expand(cext, sig)

    def square(y, carry):
        value = sig[y]
        sig2[y] = value * value
        return carry

    lax.fori_loop(0, cy, square, 0)

    loaded(2)
    loaded(3)
    for t in range(steps):
        scale = wave[t]

        def use_p(y, now, lap):
            if t < steps - 1:
                lp[t, y] = lap
            else:
                total = qf[2, y] * lap
                for u in range(1, steps - 1):
                    total = total + qf[steps + 1 - u, y] * lp[u, y]
                acc[y] = total
            step = dp[y] if t > 0 else now - pv[y]
            moved = step + sig2[y] * lap + scale * src[y]
            dp[y] = moved
            pf[t + 2, y] = now + moved

        def use_q(y, now, lap):
            step = dq[y] if t > 0 else now - qv[y]
            moved = step + sig2[y] * lap
            if t < steps - 1:
                dq[y] = moved
            qf[t + 2, y] = now + moved

        for c in range(chunks):
            arrive(p_halo(t, c))
            laplace(pf.at[t + 1], ph.at[t], c, use_p)
            start(p_halo(t + 1, c))
        hear(2 * t)
        tell(2 * t + 1)
        for c in range(chunks):
            arrive(q_halo(t, c))
            laplace(qf.at[t + 1], qh.at[t], c, use_q)
            if t < steps - 1:
                start(q_halo(t + 1, c))
        hear(2 * t + 1)
        tell(2 * t + 2)
    for i in range(2 * steps, len(reaches) + len(bits)):
        hear(i)
        tell(i + 1)

    def image(i, carry):
        at = pl.ds(pl.multiple_of(i * 8, 8), 8)
        out = [None] * (2 * pairs)
        for y in range(cy):
            value = sig[y, at, :] * (acc[y, at, :] + qf[steps + 1, y, at, :] * lp[0, y, at, :])
            for j in range(2 * pairs):
                if spline_y[y, j] != 0:
                    term = float(2.0 * spline_y[y, j]) * value
                    out[j] = term if out[j] is None else out[j] + term
        for j in range(2 * pairs):
            narrow[j, at, :] = out[j]
        return carry

    lax.fori_loop(0, cx // 8, image, 0, unroll=2)
    tall = []
    for a in range(pairs):
        high, low = split(jnp.concatenate([narrow[2 * a], narrow[2 * a + 1]], 1))
        tall.append(dot(pro_x[...], jnp.concatenate([high, low, high], 0)))
    high, low = split(jnp.concatenate(tall, 0))
    tall = dot(jnp.concatenate([high, low, high], 1), pro_z[...])
    for a in range(pairs):
        part0[a] = tall[a * ext : (a + 1) * ext]
    halfs = ext // rows

    def piece(s):
        return pl.ds(s * group // halfs, group), pl.ds(lax.rem(s, halfs) * rows, rows)

    rim_sends = []
    for d in range(n_shot):
        to = lax.rem(shot + d, n_shot)
        own = pl.ds(to * group // halfs, group)
        pair = []
        for side, (first, step) in enumerate(((cxc, 1), (0, n_tile - 1))):
            pair.append(pltpu.make_async_remote_copy(
                src_ref=part0.at[own, pl.ds(first, 2 * OV), :], dst_ref=rims.at[side, d],
                send_sem=ri_s.at[side, d], recv_sem=ri_r.at[side, d],
                device_id={"shot": to, "tile": lax.rem(tile + step, n_tile)}, device_id_type=MESH,
            ))
        rim_sends.append(pair)

    def peer_copy(source_ref, target_ref, d, ss, rr):
        return pltpu.make_async_remote_copy(
            src_ref=source_ref, dst_ref=target_ref, send_sem=ss.at[d - 1], recv_sem=rr.at[d - 1],
            device_id={"shot": lax.rem(shot + d, n_shot)}, device_id_type=MESH,
        )

    scatter = []
    for d in range(1, n_shot):
        planes, lines = piece(lax.rem(shot + d, n_shot))
        copy = peer_copy(part0.at[planes, lines, :], rs.at[d - 1], d, rs_s, rs_r)
        copy.start()
        scatter.append(copy)

    @pl.when(has_right)
    def _():
        for pair in rim_sends:
            pair[0].start()

    @pl.when(has_left)
    def _():
        for pair in rim_sends:
            pair[1].start()

    def keep_lap(y, now, lap):
        lap_last[y] = lap

    def last_lap(c):
        arrive(p_halo(steps, c))
        laplace(pf.at[steps + 1], ph.at[steps], c, keep_lap)

    for c in range(chunks // 2):
        last_lap(c)
    planes, lines = piece(shot)
    mine = part0[planes, lines, :]
    for d in range(1, n_shot):
        scatter[d - 1].wait()
        mine = mine + rs[d - 1]

    @pl.when(has_right)
    def _():
        for pair in rim_sends:
            pair[0].wait_send()
            pair[1].wait_recv()

    @pl.when(has_left)
    def _():
        for pair in rim_sends:
            pair[1].wait_send()
            pair[0].wait_recv()

    place = lax.rem(shot, halfs)
    low_rim = functools.reduce(lambda u, v: u + v, [rims[0, d] for d in range(n_shot)])
    high_rim = functools.reduce(lambda u, v: u + v, [rims[1, d] for d in range(n_shot)])
    low_rim = low_rim * jnp.where(place == 0, 1.0, 0.0).astype(F32)
    high_rim = high_rim * jnp.where(place == halfs - 1, 1.0, 0.0).astype(F32)
    none = jnp.zeros((group, rows - 2 * OV, 128), F32)
    mine = mine + jnp.concatenate([low_rim, none], 1) + jnp.concatenate([none, high_rim], 1)
    tot[shot] = mine
    gather = []
    for d in range(1, n_shot):
        copy = peer_copy(tot.at[shot], tot.at[shot], d, ag_s, ag_r)
        copy.start()
        gather.append(copy)
    squares = jnp.zeros((8, 128), F32)
    first = lax.rem(shot, halfs) * rows
    for g in range(group):
        for r in range(0, rows, 8):
            inside = jnp.logical_and(first + r >= OV, first + r < OV + cxc)
            value = mine[g, r : r + 8] * jnp.where(inside, 1.0, 0.0).astype(F32)
            squares = squares + value * mine[g, r : r + 8]
    sq_all[0] = jnp.sum(squares, axis=0, keepdims=True)
    for d in range(n_shot * n_tile - 1, 0, -1):
        pltpu.make_async_remote_copy(
            src_ref=sq_all.at[0], dst_ref=sq_all.at[d], send_sem=sq_s, recv_sem=sq_r,
            device_id={
                "shot": lax.rem(shot + d // n_tile, n_shot), "tile": lax.rem(tile + d % n_tile, n_tile)
            },
            device_id_type=MESH,
        ).start()
    last = wave[steps]
    for y in range(cy):
        base[y] = pf[steps + 1, y] + dp[y] + last * src[y]
    for c in range(chunks // 2, chunks):
        last_lap(c)
    for copy in gather:
        copy.wait()
    left_on = jnp.where(has_left, 1.0, 0.0).astype(F32)
    right_on = jnp.where(has_right, 1.0, 0.0).astype(F32)
    for a in range(pairs):
        pieces = []
        for r in range(halfs):
            flat = a * halfs + r
            pieces.append(tot[flat // group, flat % group])
        whole = pieces[0] if halfs == 1 else jnp.concatenate(pieces, 0)
        ttot[a, :OV, :] = whole[:OV] * left_on
        ttot[a, OV : OV + cxc, :] = whole[OV : OV + cxc]
        ttot[a, OV + cxc :, :] = whole[OV + cxc :] * right_on
    expand(ttot, exp_t)
    sent([p_halo(t, c) for t in range(steps + 1) for c in range(chunks)])
    sent([q_halo(t, c) for t in range(steps) for c in range(chunks)])
    others = sq_all.at[pl.ds(1, n_shot * n_tile - 1)]
    everyone = pltpu.make_async_remote_copy(
        src_ref=others, dst_ref=others, send_sem=sq_s, recv_sem=sq_r,
        device_id={"shot": across(1)}, device_id_type=MESH,
    )
    everyone.wait_send()
    everyone.wait_recv()
    cells = float(n_tile * cxc * 2 * pairs * 64)
    mean = jnp.sum(jnp.sum(sq_all[...], axis=0), axis=1, keepdims=True) / cells
    scale_out[...] = jnp.broadcast_to(1.0 / jnp.sqrt(mean + EPSILON), scale_out.shape)


def finish_kernel(base, lap_last, sig, exp_t, ttot, scale_in, direction, p_last, turned, done, dir_sem, out_sem):
    pairs = ttot.shape[0]
    cxc = direction.shape[0]
    scale = scale_in[...]
    for a in range(pairs):
        turned[:, a * 128 : (a + 1) * 128] = ttot[a, OV : OV + cxc, :] * scale
    copies = [pltpu.make_async_copy(turned, direction, dir_sem)]
    copies[0].start()
    moved = LEARN * scale
    for y in range(base.shape[0]):
        speed = sig[y] - moved * exp_t[y]
        done[y] = base[y] + speed * speed * lap_last[y]
        copies.append(pltpu.make_async_copy(done.at[y], p_last.at[:, y, :], out_sem.at[y]))
        copies[-1].start()
    for copy in copies:
        copy.wait()


def on_device(n_shot, n_tile, p_now, p_prev, adj_now, adj_next, coef_old, signs, elem_index, wavelet):
    _, cx, cy, cz = p_now.shape
    cxc, merged = coef_old.shape
    steps = wavelet.shape[0] - 1
    cyc = cy // 2
    czc = merged // cyc
    pairs = cyc // 2
    spline_y = periodic_spline(cy, cyc).astype(np.float32)
    ext = cxc + 2 * OV
    group = max(1, pairs // n_shot)
    rows = ext // max(1, n_shot // pairs)
    dims = (cx, cy, cz, cxc, pairs, steps, group, rows, CHUNKS)
    consts = [jnp.asarray(c) for c in constants(cx, cz, cxc, czc)]
    vmem = pl.BlockSpec(memory_space=pltpu.VMEM)
    hbm = pl.BlockSpec(memory_space=pltpu.HBM)
    held = lambda v: pltpu.with_memory_space_constraint(v, pltpu.HBM)
    field = (cy, cx, cz)
    buf = lambda *shape: pltpu.VMEM(shape, F32)
    sem = lambda *shape: pltpu.SemaphoreType.DMA(shape)
    like = lambda *shape: jax.ShapeDtypeStruct(shape, F32)
    state = pl.pallas_call(
        functools.partial(kernel, dims, n_shot, n_tile, spline_y),
        out_shape=(*[like(*field)] * 4, like(pairs, ext, 128), like(1, 128)),
        in_specs=[hbm] * (8 + len(consts)),
        out_specs=(vmem,) * 6,
        scratch_shapes=[
            sem(4), buf(steps + 2, *field), buf(steps + 2, *field), *[buf(*field)] * 2,
            buf(steps, *field), *[buf(*field)] * 5, buf(cyc, cx, cz),
            buf(steps + 1, 2, cy, OV, cz), buf(steps, 2, cy, OV, cz),
            buf(pairs, ext, 128), buf(cyc, cx, cz), buf(pairs, ext, 128),
            buf(2, n_shot, group, 2 * OV, 128), buf(max(1, n_shot - 1), group, rows, 128),
            buf(n_shot, group, rows, 128), buf(n_shot * n_tile, 1, 128),
            *[sem(steps + 1, CHUNKS, 2)] * 2, *[sem(steps, CHUNKS, 2)] * 2,
            sem(2), sem(2), sem(2, n_shot), sem(2, n_shot),
            *[sem(max(1, n_shot - 1))] * 4, sem(), sem(),
            pltpu.SemaphoreType.REGULAR((max(1, (n_tile - 2).bit_length()), 2)),
            pltpu.SemaphoreType.REGULAR((max(1, (n_shot - 1).bit_length()),)),
            sem(4 + len(consts)), pltpu.VMEM(signs.shape, jnp.int32), pltpu.VMEM(signs.shape, jnp.int32),
            pltpu.SMEM(wavelet.shape, F32), buf(cxc, merged),
        ]
        + [pltpu.VMEM(c.shape, c.dtype) for c in consts],
        compiler_params=pltpu.CompilerParams(
            collective_id=0, has_side_effects=True, vmem_limit_bytes=40 * 1024 * 1024
        ),
    )(
        *map(held, (p_now[0], p_prev[0], adj_now[0], adj_next[0], coef_old)),
        *map(held, (signs, elem_index.reshape(1, -1), wavelet)), *map(held, consts),
    )
    direction, p_last = pl.pallas_call(
        finish_kernel,
        out_shape=(like(cxc, merged), like(cx, cy, cz)),
        in_specs=[vmem] * 6,
        out_specs=(hbm, hbm),
        scratch_shapes=[buf(cxc, merged), buf(*field), sem(), sem(cy)],
        compiler_params=pltpu.CompilerParams(vmem_limit_bytes=12 * 1024 * 1024),
    )(*state)
    return direction, p_last[None]


def solution(mesh):
    placed = (
        P("shot", "tile", None, None),
        P("shot", "tile", None, None),
        P("shot", "tile", None, None),
        P("shot", "tile", None, None),
        P("tile", None),
        P("shot", "tile"),
        P("tile"),
        P(),
    )
    return jax.shard_map(
        functools.partial(on_device, mesh.shape["shot"], mesh.shape["tile"]),
        mesh=mesh,
        in_specs=placed,
        out_specs=(P("tile", None), P("shot", "tile", None, None)),
        check_vma=False,
    )
```

```python
import functools

import jax
import jax.numpy as jnp
import ml_dtypes
import numpy as np
from jax import lax
from jax.experimental import pallas as pl
from jax.experimental.pallas import tpu as pltpu
from jax.sharding import PartitionSpec as P

OV = 8
LEARN = 0.02
EPSILON = 1e-06
F32 = jnp.float32
BF16 = jnp.bfloat16
MESH = pl.DeviceIdType.MESH


def spectral_second(length):
    index = np.arange(length)
    number = np.minimum(index, length - index) * (2.0 * np.pi / length)
    gap = (index[:, None] - index[None, :])[:, :, None] * index[None, None, :] % length
    return np.sum(-(number * number) / length * np.cos(2.0 * np.pi / length * gap), axis=-1)


def spline_weight(offset):
    mag = np.abs(offset)
    inner = 2.0 / 3.0 - mag * mag + 0.5 * mag * mag * mag
    outer = (2.0 - mag) ** 3 / 6.0
    return np.where(mag < 1.0, inner, np.where(mag < 2.0, outer, 0.0))


def periodic_spline(fine, coarse):
    gap = np.arange(fine)[:, None] - 2 * np.arange(coarse)[None, :]
    return sum(spline_weight((gap + image * fine - 0.5) * 0.5) for image in range(-2, 3))


def halves(matrix):
    high = matrix.astype(np.float32).astype(ml_dtypes.bfloat16)
    low = (matrix - high.astype(np.float64)).astype(ml_dtypes.bfloat16)
    return high, low


def twice(block):
    out = np.zeros((2 * block.shape[0], 2 * block.shape[1]))
    out[: block.shape[0], : block.shape[1]] = block
    out[block.shape[0] :, block.shape[1] :] = block
    return out


def constants(cx, cz, cxc, czc):
    full = cx + 2 * OV
    ramp = np.sin(0.5 * np.pi * (np.arange(OV) + 0.5) / OV) ** 2
    second_x = spectral_second(full)[OV : OV + cx]
    high, low = halves(second_x[:, OV : OV + cx] - 2.0 * np.eye(cx))
    rim = np.concatenate([second_x[:, :OV] * ramp, second_x[:, OV + cx :] * ramp[::-1]], 1)
    rim_high, rim_low = halves(rim)
    core_x = np.concatenate([high, high, low], 1)
    rim_x = np.concatenate([rim_high, rim_high, rim_low, rim_low], 1)
    rim_edge = np.concatenate([rim_x[:OV], rim_x[cx - OV :]], 0)
    high, low = halves(spectral_second(cz))
    core_z = np.block([[high, low], [high, low]])
    gap = np.arange(cx)[:, None] - 2 * (np.arange(cxc + 2 * OV)[None, :] - OV)
    expand_x = spline_weight((gap - 0.5) * 0.5)
    spline_z = periodic_spline(cz, czc)
    across = lambda m: np.concatenate([*(halves(m)[:1] * 2), halves(m)[1]], 1)
    down = lambda m: np.concatenate([*(halves(m)[:1] * 2), halves(m)[1]], 0)
    return [core_x, core_z, rim_x, rim_edge, across(expand_x), down(twice(spline_z.T)), across(expand_x.T), down(twice(spline_z))]


def split(value):
    high = value.astype(BF16)
    return high, (value - high.astype(F32)).astype(BF16)


def dot(a, b):
    return jnp.dot(a, b, preferred_element_type=F32)


def kernel(
    dims, n_shot, n_tile, spline_y,
    p_now, p_prev, q_now, q_next, coef_in, signs_in, elems_in, wave_in,
    core_x_in, core_z_in, rim_x_in, rim_edge_in, exp_x_in, exp_z_in, pro_x_in, pro_z_in,
    base, lap_last, sig, exp_t, ttot, scale_out,
    raw_sem, pf, qf, pv, qv, lp, dp, dq, acc, sig2, src, wide, cp, cq, ep, eq,
    ph, qh, cext, narrow, part0, rims, rs, tot, sq_all,
    ph_s, ph_r, qh_s, qh_r, ce_s, ce_r, ri_s, ri_r, rs_s, rs_r, ag_s, ag_r, sq_s, sq_r,
    tile_sem, shot_sem, consts_sem, signs, elems, wave, coef,
    core_x, core_z, rim_x, rim_edge, exp_x, exp_z, pro_x, pro_z,
):
    cx, cy, cz, cxc, pairs, steps, group, rows = dims
    shot = lax.axis_index("shot")
    tile = lax.axis_index("tile")
    has_left = tile > 0
    has_right = tile < n_tile - 1
    ext = cxc + 2 * OV

    def across(bit):
        return shot + bit - 2 * bit * lax.rem(lax.div(shot, bit), 2)

    barrier = pltpu.get_barrier_semaphore()
    bits = [1 << b for b in range((n_shot - 1).bit_length())]
    reaches = [1 << b for b in range((n_tile - 2).bit_length())]

    def greet(right, left, reach):
        @pl.when(tile < n_tile - reach)
        def _():
            pl.semaphore_signal(
                right, inc=1, device_id={"tile": lax.rem(tile + reach, n_tile)}, device_id_type=MESH
            )

        @pl.when(tile >= reach)
        def _():
            pl.semaphore_signal(
                left, inc=1, device_id={"tile": lax.rem(tile + n_tile - reach, n_tile)}, device_id_type=MESH
            )

    greet(barrier, barrier, 1)
    for bit in bits:
        pl.semaphore_signal(barrier, inc=1, device_id={"shot": across(bit)}, device_id_type=MESH)

    def tell(i):
        if i < len(reaches):
            greet(tile_sem.at[i, 0], tile_sem.at[i, 1], reaches[i])
        elif i < len(reaches) + len(bits):
            at = i - len(reaches)
            pl.semaphore_signal(shot_sem.at[at], inc=1, device_id={"shot": across(bits[at])}, device_id_type=MESH)

    def hear(i):
        if i < len(reaches):
            @pl.when(tile >= reaches[i])
            def _():
                pl.semaphore_wait(tile_sem.at[i, 0], 1)

            @pl.when(tile < n_tile - reaches[i])
            def _():
                pl.semaphore_wait(tile_sem.at[i, 1], 1)
        elif i < len(reaches) + len(bits):
            pl.semaphore_wait(shot_sem.at[i - len(reaches)], 1)

    def load(ref, out, s):
        copy = pltpu.make_async_copy(ref, out, s)
        copy.start()
        return copy

    fields = ((p_now, pf.at[1]), (q_now, qf.at[1]), (p_prev, pv), (q_next, qv))
    matrices = (
        (coef_in, coef), (signs_in, signs), (elems_in, elems), (wave_in, wave),
        (core_x_in, core_x), (core_z_in, core_z), (rim_x_in, rim_x), (rim_edge_in, rim_edge),
        (exp_x_in, exp_x),
        (exp_z_in, exp_z), (pro_x_in, pro_x), (pro_z_in, pro_z),
    )

    def load_planes(i):
        for y in range(cy):
            pltpu.make_async_copy(fields[i][0].at[:, y, :], fields[i][1].at[y], raw_sem.at[i]).start()

    def loaded(i):
        pltpu.make_async_copy(fields[i][1], fields[i][1], raw_sem.at[i]).wait()

    load_planes(0)
    load_planes(1)
    small = [load(a, b, consts_sem.at[i]) for i, (a, b) in enumerate(matrices)]
    load_planes(2)
    load_planes(3)

    @pl.when(jnp.logical_not(has_left))
    def _():
        ph[:, 0] = jnp.zeros_like(ph[:, 0])
        qh[:, 0] = jnp.zeros_like(qh[:, 0])
        cext[:, :OV, :] = jnp.zeros((pairs, OV, 128), F32)
        rims[0] = jnp.zeros_like(rims[0])

    @pl.when(jnp.logical_not(has_right))
    def _():
        ph[:, 1] = jnp.zeros_like(ph[:, 1])
        qh[:, 1] = jnp.zeros_like(qh[:, 1])
        cext[:, OV + cxc :, :] = jnp.zeros((pairs, OV, 128), F32)
        rims[1] = jnp.zeros_like(rims[1])

    def beside(to_right, right_dst, to_left, left_dst, ss, rr):
        right = pltpu.make_async_remote_copy(
            src_ref=to_right, dst_ref=right_dst, send_sem=ss.at[0], recv_sem=rr.at[0],
            device_id={"tile": lax.rem(tile + 1, n_tile)}, device_id_type=MESH,
        )
        left = pltpu.make_async_remote_copy(
            src_ref=to_left, dst_ref=left_dst, send_sem=ss.at[1], recv_sem=rr.at[1],
            device_id={"tile": lax.rem(tile + n_tile - 1, n_tile)}, device_id_type=MESH,
        )
        return right, left

    def start(pair):
        @pl.when(has_right)
        def _():
            pair[0].start()

        @pl.when(has_left)
        def _():
            pair[1].start()

    def finish(pair):
        @pl.when(has_right)
        def _():
            pair[0].wait_send()
            pair[1].wait_recv()

        @pl.when(has_left)
        def _():
            pair[1].wait_send()
            pair[0].wait_recv()

    def field_halo(field, edges, halo, t, ss, rr):
        to_right = field.at[1, :, cx - OV :, :] if t == 0 else edges.at[t - 1, 0]
        to_left = field.at[1, :, :OV, :] if t == 0 else edges.at[t - 1, 1]
        return beside(to_right, halo.at[t, 0], to_left, halo.at[t, 1], ss.at[t], rr.at[t])

    p_halo = lambda t: field_halo(pf, ep, ph, t, ph_s, ph_r)
    q_halo = lambda t: field_halo(qf, eq, qh, t, qh_s, qh_r)

    def arrive(pair):
        @pl.when(has_right)
        def _():
            pair[1].wait_recv()

        @pl.when(has_left)
        def _():
            pair[0].wait_recv()

    def sent(pairs):
        @pl.when(has_right)
        def _():
            for pair in pairs:
                pair[0].wait_send()

        @pl.when(has_left)
        def _():
            for pair in pairs:
                pair[1].wait_send()

    beside_count = 1 - lax.div(tile + 1, n_tile) + lax.div(tile + n_tile - 1, n_tile)
    pl.semaphore_wait(barrier, len(bits) + beside_count)
    loaded(0)
    start(p_halo(0))
    loaded(1)
    start(q_halo(0))
    tell(0)
    for copy in small[:4]:
        copy.wait()
    for a in range(pairs):
        cext[a, OV : OV + cxc, :] = coef[:, a * 128 : (a + 1) * 128]
    coef_rims = beside(
        cext.at[:, cxc : cxc + OV, :], cext.at[:, :OV, :],
        cext.at[:, OV : 2 * OV, :], cext.at[:, OV + cxc :, :], ce_s, ce_r,
    )
    start(coef_rims)

    def core(y0, a, b, out):
        high, low = split(jnp.concatenate([a, b], 1))
        ox = dot(core_x[...], jnp.concatenate([high, low, high], 0))
        oz = dot(
            jnp.concatenate(
                [
                    jnp.concatenate([high[:, :cz], low[:, :cz]], 1),
                    jnp.concatenate([high[:, cz:], low[:, cz:]], 1),
                ],
                0,
            ),
            core_z[...],
        )
        oz = oz[:, :cz] + oz[:, cz:]
        out[y0] = ox[:, :cz] + oz[:cx]
        out[y0 + 1] = ox[:, cz:] + oz[cx:]

    def cores(field, out):
        for y in range(0, cy, 2):
            core(y, field[y], field[y + 1], out)

    def rim(matrix, halo, y):
        edge = jnp.concatenate(
            [
                jnp.concatenate([halo[0, y], halo[0, y + 1]], 1),
                jnp.concatenate([halo[1, y], halo[1, y + 1]], 1),
            ],
            0,
        )
        high, low = split(edge)
        return dot(matrix[...], jnp.concatenate([high, low, high, low], 0))

    def laplace(field, partial, halo, use, other=None, out=None):
        for y in range(0, cy, 2):
            a = field[y]
            b = field[y + 1]
            ox = rim(rim_x, halo, y)
            before = field[(y + cy - 1) % cy]
            after = field[(y + 2) % cy]
            if other is not None:
                core(y, other[y], other[y + 1], out)
            use(y, a, partial[y] + ox[:, :cz] + (before + b))
            use(y + 1, b, partial[y + 1] + ox[:, cz:] + (a + after))

    def edges(field, partial, halo, use, out):
        for y in range(0, cy, 2):
            ox = rim(rim_edge, halo, y)
            for side, at in ((1, slice(0, OV)), (0, slice(cx - OV, cx))):
                a = field[y, at, :]
                b = field[y + 1, at, :]
                part = ox[:OV] if side else ox[OV:]
                before = field[(y + cy - 1) % cy, at, :]
                after = field[(y + 2) % cy, at, :]
                out[side, y] = use(y, at, a, partial[y, at, :] + part[:, :cz] + (before + b))
                out[side, y + 1] = use(y + 1, at, b, partial[y + 1, at, :] + part[:, cz:] + (a + after))

    def expand(coefs, out):
        tall = []
        for a in range(0, pairs, 2):
            high, low = split(jnp.concatenate([coefs[a], coefs[a + 1]], 1))
            both = dot(exp_x[...], jnp.concatenate([high, low, high], 0))
            tall += [both[:, :128], both[:, 128:]]
        high, low = split(jnp.concatenate(tall, 0))
        both = dot(jnp.concatenate([high, low, high], 1), exp_z[...])
        for a in range(pairs):
            wide[2 * a] = both[a * cx : (a + 1) * cx, :cz]
            wide[2 * a + 1] = both[a * cx : (a + 1) * cx, cz:]

        def body(i, carry):
            at = pl.ds(pl.multiple_of(i * 8, 8), 8)
            planes = [wide[j, at, :] for j in range(2 * pairs)]
            for y in range(cy):
                terms = [
                    float(spline_y[y, j]) * planes[j] for j in range(2 * pairs) if spline_y[y, j] != 0
                ]
                out[y, at, :] = functools.reduce(lambda u, v: u + v, terms)
            return carry

        lax.fori_loop(0, cx // 8, body, 0)

    count = elems.shape[1]
    where_to = elems[...]
    amount = (2 * signs[...] - 1).astype(F32)
    row_of = lax.rem(lax.div(where_to, cz), cy) * cx + lax.div(where_to, cz * cy)
    lanes = (lax.broadcasted_iota(jnp.int32, (cz, count), 0) == lax.rem(where_to, cz)).astype(F32)
    lanes = lanes.astype(BF16)

    def source(y, carry):
        place = lax.broadcasted_iota(jnp.int32, (cx, count), 0) + y * cx
        hits = jnp.where(place == row_of, amount, 0.0).astype(BF16)
        src[y] = lax.dot_general(hits, lanes, (((1,), (1,)), ((), ())), preferred_element_type=F32)
        return carry

    lax.fori_loop(0, cy, source, 0, unroll=2)
    for copy in small[4:]:
        copy.wait()
    cores(pf.at[1], cp)
    finish(coef_rims)
    expand(cext, sig)

    def square(y, carry):
        value = sig[y]
        sig2[y] = value * value
        return carry

    lax.fori_loop(0, cy, square, 0)

    loaded(2)
    loaded(3)
    for t in range(steps):
        scale = wave[t]

        def move_p(y, at, now, lap):
            past = dp[y, at, :] if t > 0 else now - pv[y, at, :]
            return past + sig2[y, at, :] * lap + scale * src[y, at, :]

        def use_p(y, now, lap):
            if t < steps - 1:
                lp[t, y] = lap
            else:
                total = qf[2, y] * lap
                for u in range(1, steps - 1):
                    total = total + qf[steps + 1 - u, y] * lp[u, y]
                acc[y] = total
            moved = move_p(y, slice(0, cx), now, lap)
            dp[y] = moved
            pf[t + 2, y] = now + moved

        def move_q(y, at, now, lap):
            past = dq[y, at, :] if t > 0 else now - qv[y, at, :]
            return past + sig2[y, at, :] * lap

        def use_q(y, now, lap):
            moved = move_q(y, slice(0, cx), now, lap)
            if t < steps - 1:
                dq[y] = moved
            qf[t + 2, y] = now + moved

        arrive(p_halo(t))
        edges(pf.at[t + 1], cp, ph.at[t], lambda y, at, now, lap: now + move_p(y, at, now, lap), ep.at[t])
        start(p_halo(t + 1))
        laplace(pf.at[t + 1], cp, ph.at[t], use_p, qf.at[t + 1], cq)
        hear(2 * t)
        tell(2 * t + 1)
        arrive(q_halo(t))
        if t < steps - 1:
            edges(qf.at[t + 1], cq, qh.at[t], lambda y, at, now, lap: now + move_q(y, at, now, lap), eq.at[t])
            start(q_halo(t + 1))
        laplace(qf.at[t + 1], cq, qh.at[t], use_q, *(() if t == steps - 1 else (pf.at[t + 2], cp)))
        hear(2 * t + 1)
        tell(2 * t + 2)
    for i in range(2 * steps, len(reaches) + len(bits)):
        hear(i)
        tell(i + 1)

    def image(i, carry):
        at = pl.ds(pl.multiple_of(i * 8, 8), 8)
        out = [None] * (2 * pairs)
        for y in range(cy):
            value = sig[y, at, :] * (acc[y, at, :] + qf[steps + 1, y, at, :] * lp[0, y, at, :])
            for j in range(2 * pairs):
                if spline_y[y, j] != 0:
                    term = float(2.0 * spline_y[y, j]) * value
                    out[j] = term if out[j] is None else out[j] + term
        for j in range(2 * pairs):
            narrow[j, at, :] = out[j]
        return carry

    lax.fori_loop(0, cx // 8, image, 0, unroll=4)
    tall = []
    for a in range(pairs):
        high, low = split(jnp.concatenate([narrow[2 * a], narrow[2 * a + 1]], 1))
        tall.append(dot(pro_x[...], jnp.concatenate([high, low, high], 0)))
    high, low = split(jnp.concatenate(tall, 0))
    tall = dot(jnp.concatenate([high, low, high], 1), pro_z[...])
    for a in range(pairs):
        part0[a] = tall[a * ext : (a + 1) * ext]
    halfs = ext // rows

    def piece(s):
        return pl.ds(s * group // halfs, group), pl.ds(lax.rem(s, halfs) * rows, rows)

    rim_sends = []
    for d in range(n_shot):
        to = lax.rem(shot + d, n_shot)
        own = pl.ds(to * group // halfs, group)
        pair = []
        for side, (first, step) in enumerate(((cxc, 1), (0, n_tile - 1))):
            pair.append(pltpu.make_async_remote_copy(
                src_ref=part0.at[own, pl.ds(first, 2 * OV), :], dst_ref=rims.at[side, d],
                send_sem=ri_s.at[side, d], recv_sem=ri_r.at[side, d],
                device_id={"shot": to, "tile": lax.rem(tile + step, n_tile)}, device_id_type=MESH,
            ))
        rim_sends.append(pair)

    def peer_copy(source_ref, target_ref, d, ss, rr):
        return pltpu.make_async_remote_copy(
            src_ref=source_ref, dst_ref=target_ref, send_sem=ss.at[d - 1], recv_sem=rr.at[d - 1],
            device_id={"shot": lax.rem(shot + d, n_shot)}, device_id_type=MESH,
        )

    scatter = []
    for d in range(1, n_shot):
        planes, lines = piece(lax.rem(shot + d, n_shot))
        copy = peer_copy(part0.at[planes, lines, :], rs.at[d - 1], d, rs_s, rs_r)
        copy.start()
        scatter.append(copy)

    @pl.when(has_right)
    def _():
        for pair in rim_sends:
            pair[0].start()

    @pl.when(has_left)
    def _():
        for pair in rim_sends:
            pair[1].start()

    def keep_lap(y, now, lap):
        lap_last[y] = lap

    cores(pf.at[steps + 1], cp)
    planes, lines = piece(shot)
    mine = part0[planes, lines, :]
    for d in range(1, n_shot):
        scatter[d - 1].wait()
        mine = mine + rs[d - 1]

    @pl.when(has_right)
    def _():
        for pair in rim_sends:
            pair[0].wait_send()
            pair[1].wait_recv()

    @pl.when(has_left)
    def _():
        for pair in rim_sends:
            pair[1].wait_send()
            pair[0].wait_recv()

    place = lax.rem(shot, halfs)
    low_rim = functools.reduce(lambda u, v: u + v, [rims[0, d] for d in range(n_shot)])
    high_rim = functools.reduce(lambda u, v: u + v, [rims[1, d] for d in range(n_shot)])
    low_rim = low_rim * jnp.where(place == 0, 1.0, 0.0).astype(F32)
    high_rim = high_rim * jnp.where(place == halfs - 1, 1.0, 0.0).astype(F32)
    none = jnp.zeros((group, rows - 2 * OV, 128), F32)
    mine = mine + jnp.concatenate([low_rim, none], 1) + jnp.concatenate([none, high_rim], 1)
    tot[shot] = mine
    squares = jnp.zeros((8, 128), F32)
    first = lax.rem(shot, halfs) * rows
    for g in range(group):
        for r in range(0, rows, 8):
            inside = jnp.logical_and(first + r >= OV, first + r < OV + cxc)
            value = mine[g, r : r + 8] * jnp.where(inside, 1.0, 0.0).astype(F32)
            squares = squares + value * mine[g, r : r + 8]
    sq_all[0] = jnp.sum(squares, axis=0, keepdims=True)
    for d in range(n_shot * n_tile - 1, 0, -1):
        pltpu.make_async_remote_copy(
            src_ref=sq_all.at[0], dst_ref=sq_all.at[d], send_sem=sq_s, recv_sem=sq_r,
            device_id={
                "shot": lax.rem(shot + d // n_tile, n_shot), "tile": lax.rem(tile + d % n_tile, n_tile)
            },
            device_id_type=MESH,
        ).start()
    gather = []
    for d in range(1, n_shot):
        copy = peer_copy(tot.at[shot], tot.at[shot], d, ag_s, ag_r)
        copy.start()
        gather.append(copy)
    last = wave[steps]
    for y in range(cy):
        base[y] = pf[steps + 1, y] + dp[y] + last * src[y]
    arrive(p_halo(steps))
    laplace(pf.at[steps + 1], cp, ph.at[steps], keep_lap)
    for copy in gather:
        copy.wait()
    left_on = jnp.where(has_left, 1.0, 0.0).astype(F32)
    right_on = jnp.where(has_right, 1.0, 0.0).astype(F32)
    for a in range(pairs):
        pieces = []
        for r in range(halfs):
            flat = a * halfs + r
            pieces.append(tot[flat // group, flat % group])
        whole = pieces[0] if halfs == 1 else jnp.concatenate(pieces, 0)
        ttot[a, :OV, :] = whole[:OV] * left_on
        ttot[a, OV : OV + cxc, :] = whole[OV : OV + cxc]
        ttot[a, OV + cxc :, :] = whole[OV + cxc :] * right_on
    expand(ttot, exp_t)
    sent([p_halo(t) for t in range(steps + 1)])
    sent([q_halo(t) for t in range(steps)])
    others = sq_all.at[pl.ds(1, n_shot * n_tile - 1)]
    everyone = pltpu.make_async_remote_copy(
        src_ref=others, dst_ref=others, send_sem=sq_s, recv_sem=sq_r,
        device_id={"shot": across(1)}, device_id_type=MESH,
    )
    everyone.wait_send()
    everyone.wait_recv()
    cells = float(n_tile * cxc * 2 * pairs * 64)
    mean = jnp.sum(jnp.sum(sq_all[...], axis=0), axis=1, keepdims=True) / cells
    scale_out[...] = jnp.broadcast_to(1.0 / jnp.sqrt(mean + EPSILON), scale_out.shape)


def finish_kernel(base, lap_last, sig, exp_t, ttot, scale_in, direction, p_last, turned, done, dir_sem, out_sem):
    pairs = ttot.shape[0]
    cxc = direction.shape[0]
    scale = scale_in[...]
    for a in range(pairs):
        turned[:, a * 128 : (a + 1) * 128] = ttot[a, OV : OV + cxc, :] * scale
    copies = [pltpu.make_async_copy(turned, direction, dir_sem)]
    copies[0].start()
    moved = LEARN * scale
    for y in range(base.shape[0]):
        speed = sig[y] - moved * exp_t[y]
        done[y] = base[y] + speed * speed * lap_last[y]
        copies.append(pltpu.make_async_copy(done.at[y], p_last.at[:, y, :], out_sem.at[y]))
        copies[-1].start()
    for copy in copies:
        copy.wait()


def on_device(n_shot, n_tile, p_now, p_prev, adj_now, adj_next, coef_old, signs, elem_index, wavelet):
    _, cx, cy, cz = p_now.shape
    cxc, merged = coef_old.shape
    steps = wavelet.shape[0] - 1
    cyc = cy // 2
    czc = merged // cyc
    pairs = cyc // 2
    spline_y = periodic_spline(cy, cyc).astype(np.float32)
    ext = cxc + 2 * OV
    group = max(1, pairs // n_shot)
    rows = ext // max(1, n_shot // pairs)
    dims = (cx, cy, cz, cxc, pairs, steps, group, rows)
    consts = [jnp.asarray(c) for c in constants(cx, cz, cxc, czc)]
    vmem = pl.BlockSpec(memory_space=pltpu.VMEM)
    hbm = pl.BlockSpec(memory_space=pltpu.HBM)
    held = lambda v: pltpu.with_memory_space_constraint(v, pltpu.HBM)
    field = (cy, cx, cz)
    buf = lambda *shape: pltpu.VMEM(shape, F32)
    sem = lambda *shape: pltpu.SemaphoreType.DMA(shape)
    like = lambda *shape: jax.ShapeDtypeStruct(shape, F32)
    state = pl.pallas_call(
        functools.partial(kernel, dims, n_shot, n_tile, spline_y),
        out_shape=(*[like(*field)] * 4, like(pairs, ext, 128), like(1, 128)),
        in_specs=[hbm] * (8 + len(consts)),
        out_specs=(vmem,) * 6,
        scratch_shapes=[
            sem(4), buf(steps + 2, *field), buf(steps + 2, *field), *[buf(*field)] * 2,
            buf(steps, *field), *[buf(*field)] * 5, buf(cyc, cx, cz),
            *[buf(*field)] * 2, *[buf(steps, 2, cy, OV, cz)] * 2,
            buf(steps + 1, 2, cy, OV, cz), buf(steps, 2, cy, OV, cz),
            buf(pairs, ext, 128), buf(cyc, cx, cz), buf(pairs, ext, 128),
            buf(2, n_shot, group, 2 * OV, 128), buf(max(1, n_shot - 1), group, rows, 128),
            buf(n_shot, group, rows, 128), buf(n_shot * n_tile, 1, 128),
            *[sem(steps + 1, 2)] * 2, *[sem(steps, 2)] * 2,
            sem(2), sem(2), sem(2, n_shot), sem(2, n_shot),
            *[sem(max(1, n_shot - 1))] * 4, sem(), sem(),
            pltpu.SemaphoreType.REGULAR((max(1, (n_tile - 2).bit_length()), 2)),
            pltpu.SemaphoreType.REGULAR((max(1, (n_shot - 1).bit_length()),)),
            sem(4 + len(consts)), pltpu.VMEM(signs.shape, jnp.int32), pltpu.VMEM(signs.shape, jnp.int32),
            pltpu.SMEM(wavelet.shape, F32), buf(cxc, merged),
        ]
        + [pltpu.VMEM(c.shape, c.dtype) for c in consts],
        compiler_params=pltpu.CompilerParams(
            collective_id=0, has_side_effects=True, vmem_limit_bytes=40 * 1024 * 1024
        ),
    )(
        *map(held, (p_now[0], p_prev[0], adj_now[0], adj_next[0], coef_old)),
        *map(held, (signs, elem_index.reshape(1, -1), wavelet)), *map(held, consts),
    )
    direction, p_last = pl.pallas_call(
        finish_kernel,
        out_shape=(like(cxc, merged), like(cx, cy, cz)),
        in_specs=[vmem] * 6,
        out_specs=(hbm, hbm),
        scratch_shapes=[buf(cxc, merged), buf(*field), sem(), sem(cy)],
        compiler_params=pltpu.CompilerParams(vmem_limit_bytes=12 * 1024 * 1024),
    )(*state)
    return direction, p_last[None]


def solution(mesh):
    placed = (
        P("shot", "tile", None, None),
        P("shot", "tile", None, None),
        P("shot", "tile", None, None),
        P("shot", "tile", None, None),
        P("tile", None),
        P("shot", "tile"),
        P("tile"),
        P(),
    )
    return jax.shard_map(
        functools.partial(on_device, mesh.shape["shot"], mesh.shape["tile"]),
        mesh=mesh,
        in_specs=placed,
        out_specs=(P("tile", None), P("shot", "tile", None, None)),
        check_vma=False,
    )
```

```python
import functools

import jax
import jax.numpy as jnp
import ml_dtypes
import numpy as np
from jax import lax
from jax.experimental import pallas as pl
from jax.experimental.pallas import tpu as pltpu
from jax.sharding import PartitionSpec as P

OV = 8
LEARN = 0.02
EPSILON = 1e-06
F32 = jnp.float32
BF16 = jnp.bfloat16
MESH = pl.DeviceIdType.MESH


def spectral_second(length):
    index = np.arange(length)
    number = np.minimum(index, length - index) * (2.0 * np.pi / length)
    gap = (index[:, None] - index[None, :])[:, :, None] * index[None, None, :] % length
    return np.sum(-(number * number) / length * np.cos(2.0 * np.pi / length * gap), axis=-1)


def spline_weight(offset):
    mag = np.abs(offset)
    inner = 2.0 / 3.0 - mag * mag + 0.5 * mag * mag * mag
    outer = (2.0 - mag) ** 3 / 6.0
    return np.where(mag < 1.0, inner, np.where(mag < 2.0, outer, 0.0))


def periodic_spline(fine, coarse):
    gap = np.arange(fine)[:, None] - 2 * np.arange(coarse)[None, :]
    return sum(spline_weight((gap + image * fine - 0.5) * 0.5) for image in range(-2, 3))


def halves(matrix):
    high = matrix.astype(np.float32).astype(ml_dtypes.bfloat16)
    low = (matrix - high.astype(np.float64)).astype(ml_dtypes.bfloat16)
    return high, low


def twice(block):
    out = np.zeros((2 * block.shape[0], 2 * block.shape[1]))
    out[: block.shape[0], : block.shape[1]] = block
    out[block.shape[0] :, block.shape[1] :] = block
    return out


def constants(cx, cz, cxc, czc):
    full = cx + 2 * OV
    ramp = np.sin(0.5 * np.pi * (np.arange(OV) + 0.5) / OV) ** 2
    second_x = spectral_second(full)[OV : OV + cx]
    high, low = halves(second_x[:, OV : OV + cx] - 2.0 * np.eye(cx))
    rim = np.concatenate([second_x[:, :OV] * ramp, second_x[:, OV + cx :] * ramp[::-1]], 1)
    rim_high, rim_low = halves(rim)
    core_x = np.concatenate([high, high, low], 1)
    rim_x = np.concatenate([rim_high, rim_high, rim_low, rim_low], 1)
    rim_edge = np.concatenate([rim_x[:OV], rim_x[cx - OV :]], 0)
    high, low = halves(spectral_second(cz))
    core_z = np.block([[high, low], [high, low]])
    gap = np.arange(cx)[:, None] - 2 * (np.arange(cxc + 2 * OV)[None, :] - OV)
    expand_x = spline_weight((gap - 0.5) * 0.5)
    spline_z = periodic_spline(cz, czc)
    across = lambda m: np.concatenate([*(halves(m)[:1] * 2), halves(m)[1]], 1)
    down = lambda m: np.concatenate([*(halves(m)[:1] * 2), halves(m)[1]], 0)
    return [core_x, core_z, rim_x, rim_edge, across(expand_x), down(twice(spline_z.T)), across(expand_x.T), down(twice(spline_z))]


def split(value):
    high = value.astype(BF16)
    return high, (value - high.astype(F32)).astype(BF16)


def dot(a, b):
    return jnp.dot(a, b, preferred_element_type=F32)


def kernel(
    dims, n_shot, n_tile, spline_y,
    p_now, p_prev, q_now, q_next, coef_in, signs_in, elems_in, wave_in,
    core_x_in, core_z_in, rim_x_in, rim_edge_in, exp_x_in, exp_z_in, pro_x_in, pro_z_in,
    base, lap_last, sig, exp_t, ttot, scale_out,
    raw_sem, pf, qf, pv, qv, lp, dp, dq, acc, sig2, src, wide, cp, cq, ep, eq,
    ph, qh, cext, narrow, part0, rims, rs, tot, sq_all,
    ph_s, ph_r, qh_s, qh_r, ce_s, ce_r, ri_s, ri_r, rs_s, rs_r, ag_s, ag_r, sq_s, sq_r,
    tile_sem, shot_sem, consts_sem, signs, elems, wave, coef,
    core_x, core_z, rim_x, rim_edge, exp_x, exp_z, pro_x, pro_z,
):
    cx, cy, cz, cxc, pairs, steps, group, rows = dims
    shot = lax.axis_index("shot")
    tile = lax.axis_index("tile")
    has_left = tile > 0
    has_right = tile < n_tile - 1
    ext = cxc + 2 * OV

    def across(bit):
        return shot + bit - 2 * bit * lax.rem(lax.div(shot, bit), 2)

    barrier = pltpu.get_barrier_semaphore()
    bits = [1 << b for b in range((n_shot - 1).bit_length())]
    reaches = [1 << b for b in range((n_tile - 2).bit_length())]

    def greet(right, left, reach):
        @pl.when(tile < n_tile - reach)
        def _():
            pl.semaphore_signal(
                right, inc=1, device_id={"tile": lax.rem(tile + reach, n_tile)}, device_id_type=MESH
            )

        @pl.when(tile >= reach)
        def _():
            pl.semaphore_signal(
                left, inc=1, device_id={"tile": lax.rem(tile + n_tile - reach, n_tile)}, device_id_type=MESH
            )

    greet(barrier, barrier, 1)
    for bit in bits:
        pl.semaphore_signal(barrier, inc=1, device_id={"shot": across(bit)}, device_id_type=MESH)

    def tell(i):
        if i < len(reaches):
            greet(tile_sem.at[i, 0], tile_sem.at[i, 1], reaches[i])
        elif i < len(reaches) + len(bits):
            at = i - len(reaches)
            pl.semaphore_signal(shot_sem.at[at], inc=1, device_id={"shot": across(bits[at])}, device_id_type=MESH)

    def hear(i):
        if i < len(reaches):
            @pl.when(tile >= reaches[i])
            def _():
                pl.semaphore_wait(tile_sem.at[i, 0], 1)

            @pl.when(tile < n_tile - reaches[i])
            def _():
                pl.semaphore_wait(tile_sem.at[i, 1], 1)
        elif i < len(reaches) + len(bits):
            pl.semaphore_wait(shot_sem.at[i - len(reaches)], 1)

    def load(ref, out, s):
        copy = pltpu.make_async_copy(ref, out, s)
        copy.start()
        return copy

    fields = ((p_now, pf.at[1]), (q_now, qf.at[1]), (p_prev, pv), (q_next, qv))
    matrices = (
        (coef_in, coef), (signs_in, signs), (elems_in, elems), (wave_in, wave),
        (core_x_in, core_x), (core_z_in, core_z), (rim_x_in, rim_x), (rim_edge_in, rim_edge),
        (exp_x_in, exp_x),
        (exp_z_in, exp_z), (pro_x_in, pro_x), (pro_z_in, pro_z),
    )

    def load_planes(i):
        for y in range(cy):
            pltpu.make_async_copy(fields[i][0].at[:, y, :], fields[i][1].at[y], raw_sem.at[i]).start()

    def loaded(i):
        pltpu.make_async_copy(fields[i][1], fields[i][1], raw_sem.at[i]).wait()

    load_planes(0)
    load_planes(1)
    small = [load(a, b, consts_sem.at[i]) for i, (a, b) in enumerate(matrices)]
    load_planes(2)
    load_planes(3)

    @pl.when(jnp.logical_not(has_left))
    def _():
        ph[:, 0] = jnp.zeros_like(ph[:, 0])
        qh[:, 0] = jnp.zeros_like(qh[:, 0])
        cext[:, :OV, :] = jnp.zeros((pairs, OV, 128), F32)
        rims[0] = jnp.zeros_like(rims[0])

    @pl.when(jnp.logical_not(has_right))
    def _():
        ph[:, 1] = jnp.zeros_like(ph[:, 1])
        qh[:, 1] = jnp.zeros_like(qh[:, 1])
        cext[:, OV + cxc :, :] = jnp.zeros((pairs, OV, 128), F32)
        rims[1] = jnp.zeros_like(rims[1])

    def beside(to_right, right_dst, to_left, left_dst, ss, rr):
        right = pltpu.make_async_remote_copy(
            src_ref=to_right, dst_ref=right_dst, send_sem=ss.at[0], recv_sem=rr.at[0],
            device_id={"tile": lax.rem(tile + 1, n_tile)}, device_id_type=MESH,
        )
        left = pltpu.make_async_remote_copy(
            src_ref=to_left, dst_ref=left_dst, send_sem=ss.at[1], recv_sem=rr.at[1],
            device_id={"tile": lax.rem(tile + n_tile - 1, n_tile)}, device_id_type=MESH,
        )
        return right, left

    def start(pair):
        @pl.when(has_right)
        def _():
            pair[0].start()

        @pl.when(has_left)
        def _():
            pair[1].start()

    def finish(pair):
        @pl.when(has_right)
        def _():
            pair[0].wait_send()
            pair[1].wait_recv()

        @pl.when(has_left)
        def _():
            pair[1].wait_send()
            pair[0].wait_recv()

    def field_halo(field, edges, halo, t, ss, rr):
        to_right = field.at[1, :, cx - OV :, :] if t == 0 else edges.at[t - 1, 0]
        to_left = field.at[1, :, :OV, :] if t == 0 else edges.at[t - 1, 1]
        return beside(to_right, halo.at[t, 0], to_left, halo.at[t, 1], ss.at[t], rr.at[t])

    p_halo = lambda t: field_halo(pf, ep, ph, t, ph_s, ph_r)
    q_halo = lambda t: field_halo(qf, eq, qh, t, qh_s, qh_r)

    def arrive(pair):
        @pl.when(has_right)
        def _():
            pair[1].wait_recv()

        @pl.when(has_left)
        def _():
            pair[0].wait_recv()

    def sent(pairs):
        @pl.when(has_right)
        def _():
            for pair in pairs:
                pair[0].wait_send()

        @pl.when(has_left)
        def _():
            for pair in pairs:
                pair[1].wait_send()

    beside_count = 1 - lax.div(tile + 1, n_tile) + lax.div(tile + n_tile - 1, n_tile)
    pl.semaphore_wait(barrier, len(bits) + beside_count)
    loaded(0)
    start(p_halo(0))
    loaded(1)
    start(q_halo(0))
    tell(0)
    for copy in small[:4]:
        copy.wait()
    for a in range(pairs):
        cext[a, OV : OV + cxc, :] = coef[:, a * 128 : (a + 1) * 128]
    coef_rims = beside(
        cext.at[:, cxc : cxc + OV, :], cext.at[:, :OV, :],
        cext.at[:, OV : 2 * OV, :], cext.at[:, OV + cxc :, :], ce_s, ce_r,
    )
    start(coef_rims)

    def core(y0, a, b, out):
        high, low = split(jnp.concatenate([a, b], 1))
        ox = dot(core_x[...], jnp.concatenate([high, low, high], 0))
        oz = dot(
            jnp.concatenate(
                [
                    jnp.concatenate([high[:, :cz], low[:, :cz]], 1),
                    jnp.concatenate([high[:, cz:], low[:, cz:]], 1),
                ],
                0,
            ),
            core_z[...],
        )
        oz = oz[:, :cz] + oz[:, cz:]
        out[y0] = ox[:, :cz] + oz[:cx]
        out[y0 + 1] = ox[:, cz:] + oz[cx:]

    def cores(field, out):
        for y in range(0, cy, 2):
            core(y, field[y], field[y + 1], out)

    def rim(matrix, halo, y):
        edge = jnp.concatenate(
            [
                jnp.concatenate([halo[0, y], halo[0, y + 1]], 1),
                jnp.concatenate([halo[1, y], halo[1, y + 1]], 1),
            ],
            0,
        )
        high, low = split(edge)
        return dot(matrix[...], jnp.concatenate([high, low, high, low], 0))

    def laplace(field, partial, halo, use, other=None, out=None):
        for y in range(0, cy, 2):
            a = field[y]
            b = field[y + 1]
            ox = rim(rim_x, halo, y)
            before = field[(y + cy - 1) % cy]
            after = field[(y + 2) % cy]
            if other is not None:
                core(y, other[y], other[y + 1], out)
            use(y, a, partial[y] + ox[:, :cz] + (before + b))
            use(y + 1, b, partial[y + 1] + ox[:, cz:] + (a + after))

    def edges(field, partial, halo, use, out):
        for y in range(0, cy, 2):
            ox = rim(rim_edge, halo, y)
            for side, at in ((1, slice(0, OV)), (0, slice(cx - OV, cx))):
                a = field[y, at, :]
                b = field[y + 1, at, :]
                part = ox[:OV] if side else ox[OV:]
                before = field[(y + cy - 1) % cy, at, :]
                after = field[(y + 2) % cy, at, :]
                out[side, y] = use(y, at, a, partial[y, at, :] + part[:, :cz] + (before + b))
                out[side, y + 1] = use(y + 1, at, b, partial[y + 1, at, :] + part[:, cz:] + (a + after))

    def expand(coefs, out):
        tall = []
        for a in range(0, pairs, 2):
            high, low = split(jnp.concatenate([coefs[a], coefs[a + 1]], 1))
            both = dot(exp_x[...], jnp.concatenate([high, low, high], 0))
            tall += [both[:, :128], both[:, 128:]]
        high, low = split(jnp.concatenate(tall, 0))
        both = dot(jnp.concatenate([high, low, high], 1), exp_z[...])
        for a in range(pairs):
            wide[2 * a] = both[a * cx : (a + 1) * cx, :cz]
            wide[2 * a + 1] = both[a * cx : (a + 1) * cx, cz:]

        def body(i, carry):
            at = pl.ds(pl.multiple_of(i * 8, 8), 8)
            planes = [wide[j, at, :] for j in range(2 * pairs)]
            for y in range(cy):
                terms = [
                    float(spline_y[y, j]) * planes[j] for j in range(2 * pairs) if spline_y[y, j] != 0
                ]
                out[y, at, :] = functools.reduce(lambda u, v: u + v, terms)
            return carry

        lax.fori_loop(0, cx // 8, body, 0, unroll=4)

    count = elems.shape[1]
    where_to = elems[...]
    amount = (2 * signs[...] - 1).astype(F32)
    row_of = lax.rem(lax.div(where_to, cz), cy) * cx + lax.div(where_to, cz * cy)
    lanes = (lax.broadcasted_iota(jnp.int32, (cz, count), 0) == lax.rem(where_to, cz)).astype(F32)
    lanes = lanes.astype(BF16)

    def source(y, carry):
        place = lax.broadcasted_iota(jnp.int32, (cx, count), 0) + y * cx
        hits = jnp.where(place == row_of, amount, 0.0).astype(BF16)
        src[y] = lax.dot_general(hits, lanes, (((1,), (1,)), ((), ())), preferred_element_type=F32)
        return carry

    lax.fori_loop(0, cy, source, 0, unroll=4)
    for copy in small[4:]:
        copy.wait()
    cores(pf.at[1], cp)
    finish(coef_rims)
    expand(cext, sig)

    def square(y, carry):
        value = sig[y]
        sig2[y] = value * value
        return carry

    lax.fori_loop(0, cy, square, 0, unroll=4)

    loaded(2)
    loaded(3)
    for t in range(steps):
        scale = wave[t]

        def move_p(y, at, now, lap):
            past = dp[y, at, :] if t > 0 else now - pv[y, at, :]
            return past + sig2[y, at, :] * lap + scale * src[y, at, :]

        def use_p(y, now, lap):
            if t < steps - 1:
                lp[t, y] = lap
            else:
                total = qf[2, y] * lap
                for u in range(1, steps - 1):
                    total = total + qf[steps + 1 - u, y] * lp[u, y]
                acc[y] = total
            moved = move_p(y, slice(0, cx), now, lap)
            dp[y] = moved
            pf[t + 2, y] = now + moved

        def move_q(y, at, now, lap):
            past = dq[y, at, :] if t > 0 else now - qv[y, at, :]
            return past + sig2[y, at, :] * lap

        def use_q(y, now, lap):
            moved = move_q(y, slice(0, cx), now, lap)
            if t < steps - 1:
                dq[y] = moved
            qf[t + 2, y] = now + moved

        arrive(p_halo(t))
        edges(pf.at[t + 1], cp, ph.at[t], lambda y, at, now, lap: now + move_p(y, at, now, lap), ep.at[t])
        start(p_halo(t + 1))
        laplace(pf.at[t + 1], cp, ph.at[t], use_p, qf.at[t + 1], cq)
        hear(2 * t)
        tell(2 * t + 1)
        arrive(q_halo(t))
        if t < steps - 1:
            edges(qf.at[t + 1], cq, qh.at[t], lambda y, at, now, lap: now + move_q(y, at, now, lap), eq.at[t])
            start(q_halo(t + 1))
        laplace(qf.at[t + 1], cq, qh.at[t], use_q, *(() if t == steps - 1 else (pf.at[t + 2], cp)))
        hear(2 * t + 1)
        tell(2 * t + 2)
    for i in range(2 * steps, len(reaches) + len(bits)):
        hear(i)
        tell(i + 1)

    def image(i, carry):
        at = pl.ds(pl.multiple_of(i * 8, 8), 8)
        out = [None] * (2 * pairs)
        for y in range(cy):
            value = sig[y, at, :] * (acc[y, at, :] + qf[steps + 1, y, at, :] * lp[0, y, at, :])
            for j in range(2 * pairs):
                if spline_y[y, j] != 0:
                    term = float(2.0 * spline_y[y, j]) * value
                    out[j] = term if out[j] is None else out[j] + term
        for j in range(2 * pairs):
            narrow[j, at, :] = out[j]
        return carry

    lax.fori_loop(0, cx // 8, image, 0, unroll=4)
    tall = []
    for a in range(pairs):
        high, low = split(jnp.concatenate([narrow[2 * a], narrow[2 * a + 1]], 1))
        tall.append(dot(pro_x[...], jnp.concatenate([high, low, high], 0)))
    high, low = split(jnp.concatenate(tall, 0))
    tall = dot(jnp.concatenate([high, low, high], 1), pro_z[...])
    for a in range(pairs):
        part0[a] = tall[a * ext : (a + 1) * ext]
    halfs = ext // rows

    def piece(s):
        return pl.ds(s * group // halfs, group), pl.ds(lax.rem(s, halfs) * rows, rows)

    rim_sends = []
    for d in range(n_shot):
        to = lax.rem(shot + d, n_shot)
        own = pl.ds(to * group // halfs, group)
        pair = []
        for side, (first, step) in enumerate(((cxc, 1), (0, n_tile - 1))):
            pair.append(pltpu.make_async_remote_copy(
                src_ref=part0.at[own, pl.ds(first, 2 * OV), :], dst_ref=rims.at[side, d],
                send_sem=ri_s.at[side, d], recv_sem=ri_r.at[side, d],
                device_id={"shot": to, "tile": lax.rem(tile + step, n_tile)}, device_id_type=MESH,
            ))
        rim_sends.append(pair)

    def peer_copy(source_ref, target_ref, d, ss, rr):
        return pltpu.make_async_remote_copy(
            src_ref=source_ref, dst_ref=target_ref, send_sem=ss.at[d - 1], recv_sem=rr.at[d - 1],
            device_id={"shot": lax.rem(shot + d, n_shot)}, device_id_type=MESH,
        )

    scatter = []
    for d in range(1, n_shot):
        planes, lines = piece(lax.rem(shot + d, n_shot))
        copy = peer_copy(part0.at[planes, lines, :], rs.at[d - 1], d, rs_s, rs_r)
        copy.start()
        scatter.append(copy)

    @pl.when(has_right)
    def _():
        for pair in rim_sends:
            pair[0].start()

    @pl.when(has_left)
    def _():
        for pair in rim_sends:
            pair[1].start()

    def keep_lap(y, now, lap):
        lap_last[y] = lap

    cores(pf.at[steps + 1], cp)
    arrive(p_halo(steps))
    laplace(pf.at[steps + 1], cp, ph.at[steps], keep_lap)
    planes, lines = piece(shot)
    mine = part0[planes, lines, :]
    for d in range(1, n_shot):
        scatter[d - 1].wait()
        mine = mine + rs[d - 1]

    @pl.when(has_right)
    def _():
        for pair in rim_sends:
            pair[0].wait_send()
            pair[1].wait_recv()

    @pl.when(has_left)
    def _():
        for pair in rim_sends:
            pair[1].wait_send()
            pair[0].wait_recv()

    place = lax.rem(shot, halfs)
    low_rim = functools.reduce(lambda u, v: u + v, [rims[0, d] for d in range(n_shot)])
    high_rim = functools.reduce(lambda u, v: u + v, [rims[1, d] for d in range(n_shot)])
    low_rim = low_rim * jnp.where(place == 0, 1.0, 0.0).astype(F32)
    high_rim = high_rim * jnp.where(place == halfs - 1, 1.0, 0.0).astype(F32)
    none = jnp.zeros((group, rows - 2 * OV, 128), F32)
    mine = mine + jnp.concatenate([low_rim, none], 1) + jnp.concatenate([none, high_rim], 1)
    tot[shot] = mine
    gather = []
    for d in range(1, n_shot):
        copy = peer_copy(tot.at[shot], tot.at[shot], d, ag_s, ag_r)
        copy.start()
        gather.append(copy)
    squares = jnp.zeros((8, 128), F32)
    first = lax.rem(shot, halfs) * rows
    for g in range(group):
        for r in range(0, rows, 8):
            inside = jnp.logical_and(first + r >= OV, first + r < OV + cxc)
            value = mine[g, r : r + 8] * jnp.where(inside, 1.0, 0.0).astype(F32)
            squares = squares + value * mine[g, r : r + 8]
    sq_all[0] = jnp.sum(squares, axis=0, keepdims=True)
    for d in range(n_shot * n_tile - 1, 0, -1):
        pltpu.make_async_remote_copy(
            src_ref=sq_all.at[0], dst_ref=sq_all.at[d], send_sem=sq_s, recv_sem=sq_r,
            device_id={
                "shot": lax.rem(shot + d // n_tile, n_shot), "tile": lax.rem(tile + d % n_tile, n_tile)
            },
            device_id_type=MESH,
        ).start()
    last = wave[steps]
    for y in range(cy):
        base[y] = pf[steps + 1, y] + dp[y] + last * src[y]
    for copy in gather:
        copy.wait()
    left_on = jnp.where(has_left, 1.0, 0.0).astype(F32)
    right_on = jnp.where(has_right, 1.0, 0.0).astype(F32)
    for a in range(pairs):
        pieces = []
        for r in range(halfs):
            flat = a * halfs + r
            pieces.append(tot[flat // group, flat % group])
        whole = pieces[0] if halfs == 1 else jnp.concatenate(pieces, 0)
        ttot[a, :OV, :] = whole[:OV] * left_on
        ttot[a, OV : OV + cxc, :] = whole[OV : OV + cxc]
        ttot[a, OV + cxc :, :] = whole[OV + cxc :] * right_on
    expand(ttot, exp_t)
    sent([p_halo(t) for t in range(steps + 1)])
    sent([q_halo(t) for t in range(steps)])
    others = sq_all.at[pl.ds(1, n_shot * n_tile - 1)]
    everyone = pltpu.make_async_remote_copy(
        src_ref=others, dst_ref=others, send_sem=sq_s, recv_sem=sq_r,
        device_id={"shot": across(1)}, device_id_type=MESH,
    )
    everyone.wait_send()
    everyone.wait_recv()
    cells = float(n_tile * cxc * 2 * pairs * 64)
    mean = jnp.sum(jnp.sum(sq_all[...], axis=0), axis=1, keepdims=True) / cells
    scale_out[...] = jnp.broadcast_to(1.0 / jnp.sqrt(mean + EPSILON), scale_out.shape)


def finish_kernel(base, lap_last, sig, exp_t, ttot, scale_in, direction, p_last, turned, done, dir_sem, out_sem):
    pairs = ttot.shape[0]
    cxc = direction.shape[0]
    scale = scale_in[...]
    for a in range(pairs):
        turned[:, a * 128 : (a + 1) * 128] = ttot[a, OV : OV + cxc, :] * scale
    copies = [pltpu.make_async_copy(turned, direction, dir_sem)]
    copies[0].start()
    moved = LEARN * scale
    for y in range(base.shape[0]):
        speed = sig[y] - moved * exp_t[y]
        done[y] = base[y] + speed * speed * lap_last[y]
        copies.append(pltpu.make_async_copy(done.at[y], p_last.at[:, y, :], out_sem.at[y]))
        copies[-1].start()
    for copy in copies:
        copy.wait()


def on_device(n_shot, n_tile, p_now, p_prev, adj_now, adj_next, coef_old, signs, elem_index, wavelet):
    _, cx, cy, cz = p_now.shape
    cxc, merged = coef_old.shape
    steps = wavelet.shape[0] - 1
    cyc = cy // 2
    czc = merged // cyc
    pairs = cyc // 2
    spline_y = periodic_spline(cy, cyc).astype(np.float32)
    ext = cxc + 2 * OV
    group = max(1, pairs // n_shot)
    rows = ext // max(1, n_shot // pairs)
    dims = (cx, cy, cz, cxc, pairs, steps, group, rows)
    consts = [jnp.asarray(c) for c in constants(cx, cz, cxc, czc)]
    vmem = pl.BlockSpec(memory_space=pltpu.VMEM)
    hbm = pl.BlockSpec(memory_space=pltpu.HBM)
    held = lambda v: pltpu.with_memory_space_constraint(v, pltpu.HBM)
    field = (cy, cx, cz)
    buf = lambda *shape: pltpu.VMEM(shape, F32)
    sem = lambda *shape: pltpu.SemaphoreType.DMA(shape)
    like = lambda *shape: jax.ShapeDtypeStruct(shape, F32)
    state = pl.pallas_call(
        functools.partial(kernel, dims, n_shot, n_tile, spline_y),
        out_shape=(*[like(*field)] * 4, like(pairs, ext, 128), like(1, 128)),
        in_specs=[hbm] * (8 + len(consts)),
        out_specs=(vmem,) * 6,
        scratch_shapes=[
            sem(4), buf(steps + 2, *field), buf(steps + 2, *field), *[buf(*field)] * 2,
            buf(steps, *field), *[buf(*field)] * 5, buf(cyc, cx, cz),
            *[buf(*field)] * 2, *[buf(steps, 2, cy, OV, cz)] * 2,
            buf(steps + 1, 2, cy, OV, cz), buf(steps, 2, cy, OV, cz),
            buf(pairs, ext, 128), buf(cyc, cx, cz), buf(pairs, ext, 128),
            buf(2, n_shot, group, 2 * OV, 128), buf(max(1, n_shot - 1), group, rows, 128),
            buf(n_shot, group, rows, 128), buf(n_shot * n_tile, 1, 128),
            *[sem(steps + 1, 2)] * 2, *[sem(steps, 2)] * 2,
            sem(2), sem(2), sem(2, n_shot), sem(2, n_shot),
            *[sem(max(1, n_shot - 1))] * 4, sem(), sem(),
            pltpu.SemaphoreType.REGULAR((max(1, (n_tile - 2).bit_length()), 2)),
            pltpu.SemaphoreType.REGULAR((max(1, (n_shot - 1).bit_length()),)),
            sem(4 + len(consts)), pltpu.VMEM(signs.shape, jnp.int32), pltpu.VMEM(signs.shape, jnp.int32),
            pltpu.SMEM(wavelet.shape, F32), buf(cxc, merged),
        ]
        + [pltpu.VMEM(c.shape, c.dtype) for c in consts],
        compiler_params=pltpu.CompilerParams(
            collective_id=0, has_side_effects=True, vmem_limit_bytes=40 * 1024 * 1024
        ),
    )(
        *map(held, (p_now[0], p_prev[0], adj_now[0], adj_next[0], coef_old)),
        *map(held, (signs, elem_index.reshape(1, -1), wavelet)), *map(held, consts),
    )
    direction, p_last = pl.pallas_call(
        finish_kernel,
        out_shape=(like(cxc, merged), like(cx, cy, cz)),
        in_specs=[vmem] * 6,
        out_specs=(hbm, hbm),
        scratch_shapes=[buf(cxc, merged), buf(*field), sem(), sem(cy)],
        compiler_params=pltpu.CompilerParams(vmem_limit_bytes=12 * 1024 * 1024),
    )(*state)
    return direction, p_last[None]


def solution(mesh):
    placed = (
        P("shot", "tile", None, None),
        P("shot", "tile", None, None),
        P("shot", "tile", None, None),
        P("shot", "tile", None, None),
        P("tile", None),
        P("shot", "tile"),
        P("tile"),
        P(),
    )
    return jax.shard_map(
        functools.partial(on_device, mesh.shape["shot"], mesh.shape["tile"]),
        mesh=mesh,
        in_specs=placed,
        out_specs=(P("tile", None), P("shot", "tile", None, None)),
        check_vma=False,
    )
```
